512 devices in a mesh: leaf: 32 (over z, x), rows: 8 (over y), rhs: 2 (over core).
Axes of the slice: x: 4, y: 8, z: 8, core: 2. Of those that a mesh axis runs over, the one named last changes fastest.
Arguments:
- right_side: float32 [64, 128, 2048], P('leaf', 'rhs', 'rows'), may hold values from -6 to 6
- inverse_diag: bfloat16 [64, 2048, 2048], P('leaf', None, ('rows', 'rhs')), may hold values from -0.1 to 1.5, as said below
- lower_blocks: bfloat16 [64, 16, 128, 2048], P('leaf', None, None, 'rows'), may hold values from -0.0625 to 0.0625
- block_rows: int32 [64, 16], P('leaf'), may hold values from 0 to 79, as said below
Outputs:
- solved: float32 [64, 128, 2048], P('leaf', 'rhs', 'rows')
The draws below stay inside these ranges and needn't reach their ends.
Inputs may be any that keep to these rules, and one draw needn't show every extreme that they name: `inverse_diag`: in every row of an inverse block, the diagonal entry is positive and larger than every other entry of that row. `block_rows`: row i lists 16 distinct block numbers below 2048 / 128 times the depth of slot i; the first is 0, the first block of the root's rows, and the second is the last block of its parent's rows; the rows of the root and of slot 63 are not read.
All inputs are finite; a program needn't handle non-finite values.
Results may differ from the reference program's by a relative error of at most 0.004.
Values may be sent and summed in bfloat16 or wider, within the bound.
A program may use at most 64 MiB of HBM per device.

```python
import math
import jax
import jax.numpy as jnp
from jax import lax

S = 2048
BLK = 128
R = 16
LEVELS = 6
NODES = 64
NRHS = 128
N_LEAF = 32


def draw_inverse_diag(key, part):
    slot_keys = jax.random.split(key, 2 * N_LEAF)

    def single(slot_key):
        diag_key, noise_key = jax.random.split(slot_key)
        diagonal = jax.random.uniform(diag_key, (S,), jnp.float32, 0.6, 1.4)
        spread_part = jax.random.normal(noise_key, (S, S), jnp.float32) * 0.4 / math.sqrt(S)
        matrix = spread_part + jnp.diag(diagonal)
        return jnp.clip(matrix, -0.09375, 1.5).astype(jnp.bfloat16)
    return lax.map(single, slot_keys)


def draw_block_rows(key, part):
    blocks_each = S // BLK
    candidates = max(LEVELS - 1, 1) * blocks_each
    slot_ids = jnp.arange(2 * N_LEAF, dtype=jnp.int32)
    height = jnp.zeros((2 * N_LEAF,), jnp.int32)
    for power_index in range(1, LEVELS + 1):
        height = height + ((slot_ids + 1) % 2 ** power_index == 0).astype(jnp.int32)
    depth_all = LEVELS - 1 - height
    bound_now = jnp.maximum(depth_all, 1) * blocks_each
    columns = jnp.arange(candidates, dtype=jnp.int32)
    scores = jax.random.randint(key, (2 * N_LEAF, candidates), 0, 65536, dtype=jnp.int32) * candidates + columns[None, :]
    scores = jnp.where(columns[None, :] >= bound_now[:, None], scores + 2 ** 30, scores)
    active_rows = depth_all[:, None] >= 1
    forced_parent = active_rows & (columns[None, :] == depth_all[:, None] * blocks_each - 1)
    scores = jnp.where(forced_parent, -1, scores)
    forced_root = active_rows & (columns[None, :] == 0)
    scores = jnp.where(forced_root, -2, scores)
    ordering = jnp.argsort(scores, axis=1, stable=True)
    return ordering[:, :R].astype(jnp.int32)


def block_levels(own_key, shape, cuts, least, largest):
    def one(axis_at, parts):
        steps = jax.random.uniform(jax.random.fold_in(jax.random.fold_in(own_key, 6), axis_at), (parts,), jnp.float32, least / len(cuts), largest / len(cuts))
        return jnp.repeat(jnp.exp(steps), shape[axis_at] // parts).reshape((-1,) + (1,) * (len(shape) - axis_at - 1))

    level = one(*cuts[0])
    for cut in cuts[1:]:
        level = level * one(*cut)
    return level


def bell_draw(stream_key, shape, deviation, most, cuts=(), held_as=jnp.bfloat16):
    array = deviation * jax.random.normal(stream_key, shape, jnp.float32)
    if cuts:
        array = array * block_levels(stream_key, shape, cuts, -0.22, 0.18)
    return jnp.clip(array, -most, most).astype(held_as)


def setup_inputs(seed: int = 0) -> dict:
    streams_of = jax.random.split(jax.random.key(seed), 5)
    return {
        "right_side": bell_draw(streams_of[0], (NODES, NRHS, S), 1.0, 6.0, ((0, 32), (1, 2), (2, 8)), jnp.float32),
        "inverse_diag": draw_inverse_diag(jax.random.fold_in(streams_of[4], 71), 0),
        "lower_blocks": bell_draw(streams_of[2], (NODES, R, BLK, S), (4 * R * BLK) ** -0.5, 0.0625, ((0, 32), (3, 8))),
        "block_rows": draw_block_rows(jax.random.fold_in(streams_of[4], 71), 0),
    }


def reference(right_side, inverse_diag, lower_blocks, block_rows):
    top_depth = LEVELS - 1
    blocks_each = S // BLK
    solved = [None] * (2 * N_LEAF)
    rounded = [None] * (2 * N_LEAF)
    for depth_now in range(LEVELS):
        height = top_depth - depth_now
        for position in range(2 ** depth_now):
            node_id = (2 * position + 1) * 2 ** height - 1
            if depth_now > 0:
                pieces = []
                for upper_depth in range(depth_now):
                    above_pos = position >> (depth_now - upper_depth)
                    pieces.append(rounded[(2 * above_pos + 1) * 2 ** (top_depth - upper_depth) - 1])
                joined = jnp.concatenate(pieces, axis=1)
                tile_view = joined.reshape(NRHS, depth_now * blocks_each, BLK)
                picked = jnp.take(tile_view, block_rows[node_id], axis=1, mode="clip").reshape(NRHS, R * BLK)
                offset = jnp.dot(picked, lower_blocks[node_id].reshape(R * BLK, S), preferred_element_type=jnp.float32)
                reduced = (right_side[node_id] - offset).astype(jnp.bfloat16)
            else:
                reduced = right_side[node_id].astype(jnp.bfloat16)
            result = jnp.dot(reduced, inverse_diag[node_id], preferred_element_type=jnp.float32)
            solved[node_id] = result
            rounded[node_id] = result.astype(jnp.bfloat16)
    solved[2 * N_LEAF - 1] = jnp.zeros((NRHS, S), jnp.float32)
    return jnp.stack(solved)
```

```python
import jax
import jax.numpy as jnp
from jax import lax
from jax.experimental import pallas as pl
from jax.experimental.pallas import tpu as pltpu
from jax.sharding import PartitionSpec as P

MESH = pl.DeviceIdType.MESH
BF16 = jnp.bfloat16
F32 = jnp.float32
RING = 8
FAR_FIRST = (4, 3, 5, 2, 6, 1, 7, 0)


def device(leaf, row, core):
    return {"leaf": leaf, "rows": row, "rhs": core}


def remote(source, target, sent, arrived, where):
    return pltpu.make_async_remote_copy(
        source, target, sent, arrived, device_id=where, device_id_type=MESH
    )


def kernel(
    block_rows, right_side, inverse_diag, lower_blocks, out,
    rhs, inv, low, anc_up, anc_lo, red, piece, result,
    load_sem, half_send, half_recv, red_send, red_recv, piece_send, piece_recv,
    pass_send, pass_recv, out_sem,
):
    leaf = lax.axis_index("leaf")
    row = lax.axis_index("rows")
    core = lax.axis_index("rhs")
    has_upper = leaf < 31
    even = leaf % 2 == 0
    trail = jnp.int32(0)
    for power in range(1, 5):
        trail = trail + ((leaf + 1) % 2**power == 0).astype(jnp.int32)
    depth = 4 - trail
    span = jnp.where(trail == 0, 1, jnp.where(trail == 1, 2, jnp.where(trail == 2, 4, jnp.where(trail == 3, 8, 16))))
    parent = jnp.where((leaf // (2 * span)) % 2 == 0, leaf + span, leaf - span)
    child_a = leaf - span // 2
    child_b = leaf + span // 2
    below_root = jnp.logical_and(has_upper, depth >= 1)
    splits = jnp.logical_and(has_upper, depth <= 3)
    sibling = jnp.where(even, leaf + 1, leaf - 1)

    loads = []
    for slot in (1, 0):
        loads.append(pltpu.make_async_copy(right_side.at[slot], rhs.at[slot], load_sem.at[slot, 0]))
        own = inv.at[slot, :, pl.ds(pl.multiple_of(core * 128, 128), 128)]
        loads.append(pltpu.make_async_copy(inverse_diag.at[slot], own, load_sem.at[slot, 1]))
        loads.append(pltpu.make_async_copy(lower_blocks.at[slot], low.at[slot], load_sem.at[slot, 2]))
    for copy in loads:
        copy.start()

    barrier = pltpu.get_barrier_semaphore()

    def greet(where):
        pl.semaphore_signal(barrier, inc=1, device_id=where, device_id_type=MESH)

    for step in range(1, RING):
        greet(device(leaf, (row + step) % RING, core))
    greet(device(leaf, row, 1 - core))
    for step in range(RING):
        greet(device(sibling, (row + step) % RING, core))

    @pl.when(below_root)
    def _():
        for step in range(RING):
            greet(device(parent, (row + step) % RING, core))

    @pl.when(splits)
    def _():
        for step in range(RING):
            greet(device(child_a, (row + step) % RING, core))
            greet(device(child_b, (row + step) % RING, core))

    pl.semaphore_wait(
        barrier,
        16 + 8 * below_root.astype(jnp.int32) + 16 * splits.astype(jnp.int32),
    )

    halves = []
    for slot in (1, 0):
        there = inv.at[slot, :, pl.ds(pl.multiple_of(core * 128, 128), 128)]
        copy = remote(
            inverse_diag.at[slot], there, half_send.at[slot], half_recv.at[slot],
            device(leaf, row, 1 - core),
        )
        copy.start()
        halves.append(copy)

    def offset_of(slot, ancestors, limit):
        picked = jnp.concatenate(
            [ancestors[jnp.clip(block_rows[slot, r], 0, limit)] for r in range(16)], axis=1
        )
        return jnp.dot(picked, low[slot].reshape(2048, 256), preferred_element_type=F32)

    def reduce_and_solve(slot, reduced):
        mine = pl.ds(2 * row, 2)
        rounded = reduced.astype(BF16)
        red[slot, 2 * row] = rounded[:, :128]
        red[slot, 2 * row + 1] = rounded[:, 128:]
        copies = []
        for step in FAR_FIRST[:-1]:
            copy = remote(
                red.at[slot, mine], red.at[slot, mine],
                red_send.at[slot, step], red_recv.at[slot, step],
                device(leaf, (row + step) % RING, core),
            )
            copy.start()
            copies.append(copy)
        for copy in copies:
            copy.wait_recv()
        full = jnp.concatenate([red[slot, b] for b in range(16)], axis=1)
        return jnp.dot(full, inv[slot], preferred_element_type=F32)

    def finish_sends(slot):
        for step in range(1, RING):
            remote(
                red.at[slot, pl.ds(2 * row, 2)], red.at[slot, pl.ds(2 * row, 2)],
                red_send.at[slot, step], red_recv.at[slot, step],
                device(leaf, (row + step) % RING, core),
            ).wait_send()

    def hand_on(level, child, which):
        level_blocks = pl.ds(16 * level, 16)
        return remote(
            anc_up.at[level_blocks], anc_up.at[level_blocks],
            pass_send.at[level, which], pass_recv.at[level],
            device(child, row, core),
        )

    def hand_across(level):
        level_blocks = pl.ds(16 * level, 16)
        return remote(
            anc_up.at[level_blocks], anc_lo.at[level_blocks],
            pass_send.at[level, 2], pass_recv.at[level + 4],
            device(sibling, row, core),
        )

    def piece_copy(child, step, which, ancestors, group):
        return remote(
            piece, ancestors.at[pl.ds(16 * depth + 2 * row, 2)],
            piece_send.at[which, step], piece_recv.at[group, step],
            device(child, (row + step) % RING, core),
        )

    crosses_all = leaf % 4 == 2

    for level in range(3):
        @pl.when(jnp.logical_and(below_root, level < depth - 1))
        def _():
            hand_on(level, parent, 0).wait_recv()

            @pl.when(splits)
            def _():
                hand_on(level, child_a, 0).start()
                hand_on(level, child_b, 1).start()

            @pl.when(crosses_all)
            def _():
                hand_across(level).start()

    loads[0].wait()
    loads[1].wait()
    loads[2].wait()
    halves[0].wait_recv()

    @pl.when(below_root)
    def _():
        for step in FAR_FIRST:
            remote(
                piece, anc_up.at[pl.ds(0, 2)], piece_send.at[0, step], piece_recv.at[0, step],
                device(parent, row, core),
            ).wait_recv()

    @pl.when(has_upper)
    def _():
        @pl.when(below_root)
        def _():
            rhs[1] = rhs[1] - offset_of(1, anc_up, 63)

        solved = reduce_and_solve(1, rhs[1])
        result[1] = solved
        rounded = solved.astype(BF16)
        piece[0] = rounded[:, :128]
        piece[1] = rounded[:, 128:]

        @pl.when(splits)
        def _():
            for step in FAR_FIRST:
                piece_copy(child_a, step, 0, anc_up, 0).start()
                piece_copy(child_b, step, 1, anc_up, 0).start()

            for level in range(3):
                @pl.when(level == depth - 1)
                def _():
                    hand_on(level, child_a, 0).start()
                    hand_on(level, child_b, 1).start()

        @pl.when(even)
        def _():
            for step in FAR_FIRST:
                piece_copy(sibling, step, 1, anc_lo, 1).start()
                if step:
                    piece_copy(leaf, step, 0, anc_lo, 1).start()
            anc_lo[64 + 2 * row] = rounded[:, :128]
            anc_lo[64 + 2 * row + 1] = rounded[:, 128:]
            hand_across(3).start()
            for block in range(64):
                anc_lo[block] = anc_up[block]

    @pl.when(leaf == 31)
    def _():
        result[1] = jnp.zeros_like(result[1])

    upper_out = pltpu.make_async_copy(result.at[1], out.at[1], out_sem.at[1])
    upper_out.start()

    loads[3].wait()
    loads[4].wait()
    loads[5].wait()
    halves[1].wait_recv()

    @pl.when(leaf % 4 == 1)
    def _():
        for block in range(48):
            anc_lo[block] = anc_up[block]

    @pl.when(leaf % 4 == 3)
    def _():
        for level in range(3):
            hand_across(level).wait_recv()

    @pl.when(jnp.logical_not(even))
    def _():
        hand_across(3).wait_recv()
        remote(
            piece, anc_lo.at[pl.ds(0, 2)], piece_send.at[0, 0], piece_recv.at[1, 0],
            device(sibling, row, core),
        ).wait_recv()

    for step in FAR_FIRST[:-1]:
        remote(
            piece, anc_lo.at[pl.ds(0, 2)], piece_send.at[0, step], piece_recv.at[1, step],
            device(sibling, row, core),
        ).wait_recv()

    solved_lower = reduce_and_solve(0, rhs[0] - offset_of(0, anc_lo, 79))
    result[0] = solved_lower
    lower_out = pltpu.make_async_copy(result.at[0], out.at[0], out_sem.at[0])
    lower_out.start()

    for copy in halves:
        copy.wait_send()
    finish_sends(0)

    @pl.when(has_upper)
    def _():
        finish_sends(1)

        @pl.when(splits)
        def _():
            for step in range(RING):
                piece_copy(child_a, step, 0, anc_up, 0).wait_send()
                piece_copy(child_b, step, 1, anc_up, 0).wait_send()
            for level in range(3):
                @pl.when(level < depth)
                def _():
                    hand_on(level, child_a, 0).wait_send()
                    hand_on(level, child_b, 1).wait_send()

        @pl.when(even)
        def _():
            for step in range(RING):
                piece_copy(sibling, step, 1, anc_lo, 1).wait_send()
                if step:
                    piece_copy(leaf, step, 0, anc_lo, 1).wait_send()
            hand_across(3).wait_send()

        @pl.when(crosses_all)
        def _():
            for level in range(3):
                hand_across(level).wait_send()

    upper_out.wait()
    lower_out.wait()


def local(right_side, inverse_diag, lower_blocks, block_rows):
    anywhere = pl.BlockSpec(memory_space=pl.ANY)
    dma = pltpu.SemaphoreType.DMA
    return pl.pallas_call(
        kernel,
        name="sweep",
        out_shape=jax.ShapeDtypeStruct((2, 64, 256), F32),
        in_specs=[pl.BlockSpec(memory_space=pltpu.SMEM), anywhere, anywhere, anywhere],
        out_specs=anywhere,
        scratch_shapes=[
            pltpu.VMEM((2, 64, 256), F32),
            pltpu.VMEM((2, 2048, 256), BF16),
            pltpu.VMEM((2, 16, 128, 256), BF16),
            pltpu.VMEM((64, 64, 128), BF16),
            pltpu.VMEM((80, 64, 128), BF16),
            pltpu.VMEM((2, 16, 64, 128), BF16),
            pltpu.VMEM((2, 64, 128), BF16),
            pltpu.VMEM((2, 64, 256), F32),
            dma((2, 3)),
            dma((2,)),
            dma((2,)),
            dma((2, 8)),
            dma((2, 8)),
            dma((2, 8)),
            dma((2, 8)),
            dma((4, 3)),
            dma((8,)),
            dma((2,)),
        ],
        compiler_params=pltpu.CompilerParams(
            collective_id=0, has_side_effects=True, vmem_limit_bytes=56 * 2**20
        ),
    )(block_rows, right_side, inverse_diag, lower_blocks)


def solution(mesh):
    return jax.shard_map(
        local,
        mesh=mesh,
        in_specs=(
            P("leaf", "rhs", "rows"),
            P("leaf", None, ("rows", "rhs")),
            P("leaf", None, None, "rows"),
            P("leaf", None),
        ),
        out_specs=P("leaf", "rhs", "rows"),
        check_vma=False,
    )
```

```python
import jax
import jax.numpy as jnp
from jax import lax
from jax.experimental import pallas as pl
from jax.experimental.pallas import tpu as pltpu
from jax.sharding import PartitionSpec as P

MESH = pl.DeviceIdType.MESH
BF16 = jnp.bfloat16
F32 = jnp.float32
RING = 8
LEVELS = 5
CHUNKS = 2
ROWS = 32
FAR_FIRST = (4, 3, 5, 2, 6, 1, 7)


def device(leaf, row, core):
    return {"leaf": leaf, "rows": row, "rhs": core}


def remote(source, target, sent, arrived, where):
    return pltpu.make_async_remote_copy(
        source, target, sent, arrived, device_id=where, device_id_type=MESH
    )


def depth_of(leaf):
    trail = jnp.int32(0)
    for power in range(1, 6):
        trail = trail + ((leaf + 1) % 2**power == 0).astype(jnp.int32)
    return 4 - trail


def kernel(
    block_rows, right_side, inverse_diag, lower_blocks, out,
    rhs, inv, low, anc_0, anc_1, red, result,
    load_sem, half_send, half_recv, red_send, red_recv, hop_send, hop_recv,
    ring_send, ring_recv, out_sem,
):
    anc = (anc_0, anc_1)
    leaf = lax.axis_index("leaf")
    row = lax.axis_index("rows")
    core = lax.axis_index("rhs")
    even = leaf % 2 == 0
    depth = depth_of(leaf)
    half_span = jnp.int32(0)
    for level in range(4):
        half_span = half_span + jnp.where(depth == level, 2 ** (3 - level), 0)
    span = jnp.maximum(2 * half_span, 1)
    parent = jnp.where((leaf // (2 * span)) % 2 == 0, leaf + span, leaf - span)
    child_a = leaf - half_span
    child_b = leaf + half_span
    has_upper = depth >= 0
    below_root = depth >= 1
    splits = jnp.logical_and(has_upper, depth <= 3)
    sibling = jnp.where(even, leaf + 1, leaf - 1)
    sibling_depth = depth_of(sibling)
    mine_cols = pl.ds(pl.multiple_of(core * 128, 128), 128)

    loads = {}
    for slot in (1, 0):
        loads[slot, 0] = pltpu.make_async_copy(right_side.at[slot], rhs.at[slot], load_sem.at[slot, 0])
        loads[slot, 1] = pltpu.make_async_copy(
            inverse_diag.at[slot], inv.at[slot, :, mine_cols], load_sem.at[slot, 1]
        )
        loads[slot, 2] = pltpu.make_async_copy(lower_blocks.at[slot], low.at[slot], load_sem.at[slot, 2])
    for copy in loads.values():
        copy.start()

    barrier = pltpu.get_barrier_semaphore()

    def greet(where):
        pl.semaphore_signal(barrier, inc=1, device_id=where, device_id_type=MESH)

    for step in FAR_FIRST:
        greet(device(leaf, (row + step) % RING, core))
    greet(device(leaf, row, 1 - core))
    greet(device(sibling, row, core))

    @pl.when(below_root)
    def _():
        greet(device(parent, row, core))

    @pl.when(splits)
    def _():
        greet(device(child_a, row, core))
        greet(device(child_b, row, core))

    pl.semaphore_wait(
        barrier, 9 + below_root.astype(jnp.int32) + 2 * splits.astype(jnp.int32)
    )

    halves = {
        slot: remote(
            inverse_diag.at[slot], inv.at[slot, :, mine_cols], half_send.at[slot], half_recv.at[slot],
            device(leaf, row, 1 - core),
        )
        for slot in (1, 0)
    }

    def ring_copies(level, chunk):
        piece = anc[chunk].at[pl.ds(16 * level + 2 * row, 2)]
        return [
            remote(
                piece, piece, ring_send.at[level, chunk, step], ring_recv.at[level, chunk, step],
                device(leaf, (row + step) % RING, core),
            )
            for step in FAR_FIRST
        ]

    def red_copies(slot, chunk):
        piece = red.at[slot, chunk, pl.ds(2 * row, 2)]
        return [
            remote(
                piece, piece, red_send.at[slot, chunk, step], red_recv.at[slot, chunk, step],
                device(leaf, (row + step) % RING, core),
            )
            for step in FAR_FIRST
        ]

    def hop(level, chunk, where, which):
        piece = anc[chunk].at[pl.ds(16 * level + 2 * row, 2)]
        return remote(
            piece, piece, hop_send.at[level, chunk, which], hop_recv.at[level, chunk],
            device(where, row, core),
        )

    def each_hop(level, chunk, act):
        @pl.when(jnp.logical_and(splits, depth >= level))
        def _():
            act(hop(level, chunk, child_a, 0))
            act(hop(level, chunk, child_b, 1))

        @pl.when(jnp.logical_and(even, sibling_depth < level))
        def _():
            act(hop(level, chunk, sibling, 0))

    def start(copy):
        copy.start()

    def spread(level, chunk):
        each_hop(level, chunk, start)
        for copy in ring_copies(level, chunk):
            copy.start()

    def wait_ring(level, chunk):
        for copy in ring_copies(level, chunk):
            copy.wait_recv()

    def set_reduced(slot, chunk, offset):
        span_rows = pl.ds(ROWS * chunk, ROWS)
        value = rhs[slot, span_rows]
        if offset is not None:
            value = value - offset
        rounded = value.astype(BF16)
        red[slot, chunk, 2 * row] = rounded[:, :128]
        red[slot, chunk, 2 * row + 1] = rounded[:, 128:]
        for copy in red_copies(slot, chunk):
            copy.start()

    def offset_of(slot, chunk, limit):
        picked = jnp.concatenate(
            [anc[chunk][jnp.clip(block_rows[slot, r], 0, limit)] for r in range(16)], axis=1
        )
        return jnp.dot(picked, low[slot].reshape(2048, 256), preferred_element_type=F32)

    def solve(slot, chunk):
        for copy in red_copies(slot, chunk):
            copy.wait_recv()
        full = jnp.concatenate([red[slot, chunk, b] for b in range(16)], axis=1)
        solved = jnp.dot(full, inv[slot], preferred_element_type=F32)
        result[slot, pl.ds(ROWS * chunk, ROWS)] = solved
        return solved

    def wait_weights(slot):
        loads[slot, 1].wait()
        halves[slot].wait_recv()

    loads[1, 0].wait()

    for level in range(LEVELS):
        @pl.when(depth != level)
        def _():
            if level == 0:
                halves[1].start()
                halves[0].start()
            for chunk in range(CHUNKS):
                hop(level, chunk, leaf, 0).wait_recv()
                spread(level, chunk)

        @pl.when(depth == level)
        def _():
            if level > 0:
                loads[1, 2].wait()
            for chunk in range(CHUNKS):
                for above in range(level):
                    wait_ring(above, chunk)
                set_reduced(1, chunk, offset_of(1, chunk, 16 * level - 1) if level else None)
            if level == 0:
                halves[1].start()
                halves[0].start()
            wait_weights(1)
            for chunk in range(CHUNKS):
                rounded = solve(1, chunk).astype(BF16)
                anc[chunk][16 * level + 2 * row] = rounded[:, :128]
                anc[chunk][16 * level + 2 * row + 1] = rounded[:, 128:]
                spread(level, chunk)
            if level == 0:
                loads[1, 2].wait()

    @pl.when(depth < 0)
    def _():
        wait_weights(1)
        loads[1, 2].wait()
        result[1] = jnp.zeros_like(result[1])

    upper_out = pltpu.make_async_copy(result.at[1], out.at[1], out_sem.at[1])
    upper_out.start()

    loads[0, 0].wait()
    loads[0, 2].wait()
    wait_weights(0)
    for chunk in range(CHUNKS):
        for level in range(LEVELS):
            @pl.when(depth <= level)
            def _():
                wait_ring(level, chunk)

        set_reduced(0, chunk, offset_of(0, chunk, 79))
    for chunk in range(CHUNKS):
        solve(0, chunk)
    lower_out = pltpu.make_async_copy(result.at[0], out.at[0], out_sem.at[0])
    lower_out.start()

    halves[1].wait_send()
    halves[0].wait_send()

    def wait_send(copy):
        copy.wait_send()

    for chunk in range(CHUNKS):
        for level in range(LEVELS):
            each_hop(level, chunk, wait_send)
            for copy in ring_copies(level, chunk):
                copy.wait_send()
        for copy in red_copies(0, chunk):
            copy.wait_send()

        @pl.when(has_upper)
        def _():
            for copy in red_copies(1, chunk):
                copy.wait_send()

    upper_out.wait()
    lower_out.wait()


def local(right_side, inverse_diag, lower_blocks, block_rows):
    anywhere = pl.BlockSpec(memory_space=pl.ANY)
    dma = pltpu.SemaphoreType.DMA
    return pl.pallas_call(
        kernel,
        name="sweep",
        out_shape=jax.ShapeDtypeStruct((2, 64, 256), F32),
        in_specs=[pl.BlockSpec(memory_space=pltpu.SMEM), anywhere, anywhere, anywhere],
        out_specs=anywhere,
        scratch_shapes=[
            pltpu.VMEM((2, 64, 256), F32),
            pltpu.VMEM((2, 2048, 256), BF16),
            pltpu.VMEM((2, 16, 128, 256), BF16),
            pltpu.VMEM((80, ROWS, 128), BF16),
            pltpu.VMEM((80, ROWS, 128), BF16),
            pltpu.VMEM((2, CHUNKS, 16, ROWS, 128), BF16),
            pltpu.VMEM((2, 64, 256), F32),
            dma((2, 3)),
            dma((2,)),
            dma((2,)),
            dma((2, CHUNKS, 8)),
            dma((2, CHUNKS, 8)),
            dma((LEVELS, CHUNKS, 2)),
            dma((LEVELS, CHUNKS)),
            dma((LEVELS, CHUNKS, 8)),
            dma((LEVELS, CHUNKS, 8)),
            dma((2,)),
        ],
        compiler_params=pltpu.CompilerParams(
            collective_id=0, has_side_effects=True, vmem_limit_bytes=56 * 2**20
        ),
    )(block_rows, right_side, inverse_diag, lower_blocks)


def solution(mesh):
    return jax.shard_map(
        local,
        mesh=mesh,
        in_specs=(
            P("leaf", "rhs", "rows"),
            P("leaf", None, ("rows", "rhs")),
            P("leaf", None, None, "rows"),
            P("leaf", None),
        ),
        out_specs=P("leaf", "rhs", "rows"),
        check_vma=False,
    )
```

```python
import jax
import jax.numpy as jnp
from jax import lax
from jax.experimental import pallas as pl
from jax.experimental.pallas import tpu as pltpu
from jax.sharding import PartitionSpec as P

MESH = pl.DeviceIdType.MESH
BF16 = jnp.bfloat16
F32 = jnp.float32
RING = 8
LEVELS = 5
CHUNKS = 2
ROWS = 32
FAR_FIRST = (4, 3, 5, 2, 6, 1, 7)


def device(leaf, row, core):
    return {"leaf": leaf, "rows": row, "rhs": core}


def remote(source, target, sent, arrived, where):
    return pltpu.make_async_remote_copy(
        source, target, sent, arrived, device_id=where, device_id_type=MESH
    )


def depth_of(leaf):
    trail = jnp.int32(0)
    for power in range(1, 6):
        trail = trail + ((leaf + 1) % 2**power == 0).astype(jnp.int32)
    return 4 - trail


def kernel(
    block_rows_in, right_side, inverse_diag, lower_blocks, out,
    block_rows, rhs, inv, low, anc_0, anc_1, red, result,
    load_sem, half_send, half_recv, red_send, red_recv, hop_send, hop_recv,
    ring_send, ring_recv, direct_send, out_sem, rows_sem, ready,
):
    anc = (anc_0, anc_1)
    leaf = lax.axis_index("leaf")
    row = lax.axis_index("rows")
    core = lax.axis_index("rhs")
    even = leaf % 2 == 0
    depth = depth_of(leaf)
    half_span = jnp.int32(0)
    for level in range(4):
        half_span = half_span + jnp.where(depth == level, 2 ** (3 - level), 0)
    span = jnp.maximum(2 * half_span, 1)
    parent = jnp.where((leaf // (2 * span)) % 2 == 0, leaf + span, leaf - span)
    child_a = leaf - half_span
    child_b = leaf + half_span
    has_upper = depth >= 0
    below_root = depth >= 1
    splits = jnp.logical_and(has_upper, depth <= 3)
    sibling = jnp.where(even, leaf + 1, leaf - 1)
    sibling_depth = depth_of(sibling)
    mine_cols = pl.ds(pl.multiple_of(core * 128, 128), 128)

    barrier = pltpu.get_barrier_semaphore()

    def greet(where):
        pl.semaphore_signal(barrier, inc=1, device_id=where, device_id_type=MESH)

    def report(where):
        pl.semaphore_signal(ready, inc=1, device_id=where, device_id_type=MESH)

    for step in FAR_FIRST:
        greet(device(leaf, (row + step) % RING, core))
    greet(device(leaf, row, 1 - core))

    @pl.when(depth == 3)
    def _():
        for step in range(RING):
            greet(device(child_a, (row + step) % RING, core))
            greet(device(child_b, (row + step) % RING, core))

    @pl.when(jnp.logical_and(has_upper, depth <= 2))
    def _():
        greet(device(child_a, row, core))
        greet(device(child_b, row, core))

    @pl.when(even)
    def _():
        for step in range(RING):
            greet(device(sibling, (row + step) % RING, core))

    block_rows_copy = pltpu.make_async_copy(block_rows_in, block_rows, rows_sem.at[0])
    loads = {}
    for slot in (1, 0):
        loads[slot, 0] = pltpu.make_async_copy(right_side.at[slot], rhs.at[slot], load_sem.at[slot, 0])
        loads[slot, 1] = pltpu.make_async_copy(
            inverse_diag.at[slot], inv.at[slot, :, mine_cols], load_sem.at[slot, 1]
        )
        loads[slot, 2] = pltpu.make_async_copy(lower_blocks.at[slot], low.at[slot], load_sem.at[slot, 2])
    for copy in loads.values():
        copy.start()
    block_rows_copy.start()

    from_parent = jnp.where(depth == 4, 8, jnp.where(below_root, 1, 0))
    pl.semaphore_wait(barrier, 8 + from_parent + jnp.where(even, 0, 8))

    @pl.when(depth == 4)
    def _():
        for step in range(RING):
            report(device(parent, (row + step) % RING, core))

    @pl.when(jnp.logical_and(below_root, depth <= 3))
    def _():
        report(device(parent, row, core))

    @pl.when(jnp.logical_not(even))
    def _():
        for step in range(RING):
            report(device(sibling, (row + step) % RING, core))

    def wait_ready():
        @pl.when(has_upper)
        def _():
            pl.semaphore_wait(ready, jnp.where(even, 8, jnp.where(depth == 3, 16, 2)))

    halves = {
        slot: remote(
            inverse_diag.at[slot], inv.at[slot, :, mine_cols], half_send.at[slot], half_recv.at[slot],
            device(leaf, row, 1 - core),
        )
        for slot in (1, 0)
    }

    def ring_copies(level, chunk):
        piece = anc[chunk].at[pl.ds(16 * level + 2 * row, 2)]
        return [
            remote(
                piece, piece, ring_send.at[level, chunk, step], ring_recv.at[level, chunk, step],
                device(leaf, (row + step) % RING, core),
            )
            for step in FAR_FIRST
        ]

    def red_copies(slot, chunk):
        piece = red.at[slot, chunk, pl.ds(2 * row, 2)]
        return [
            remote(
                piece, piece, red_send.at[slot, chunk, step], red_recv.at[slot, chunk, step],
                device(leaf, (row + step) % RING, core),
            )
            for step in FAR_FIRST
        ]

    def hop(level, chunk, where, which):
        piece = anc[chunk].at[pl.ds(16 * level + 2 * row, 2)]
        return remote(
            piece, piece, hop_send.at[level, chunk, which], hop_recv.at[level, chunk],
            device(where, row, core),
        )

    def direct(chunk, where, which, step):
        level = jnp.maximum(depth, 0)
        piece = anc[chunk].at[pl.ds(16 * level + 2 * row, 2)]
        arrived = ring_recv.at[level, chunk, step] if step else hop_recv.at[level, chunk]
        return remote(
            piece, piece, direct_send.at[chunk, which, step], arrived,
            device(where, (row + step) % RING, core),
        )

    def each_hop(level, chunk, act):
        @pl.when(jnp.logical_and(splits, jnp.logical_and(depth >= level, jnp.logical_or(depth > level, depth < 3))))
        def _():
            act(hop(level, chunk, child_a, 0))
            act(hop(level, chunk, child_b, 1))

        if level < 4:
            @pl.when(jnp.logical_and(even, sibling_depth < level))
            def _():
                act(hop(level, chunk, sibling, 0))

        if level == 3:
            @pl.when(depth == 3)
            def _():
                for step in (*FAR_FIRST, 0):
                    act(direct(chunk, child_a, 0, step))
                    act(direct(chunk, child_b, 1, step))

        if level == 4:
            @pl.when(even)
            def _():
                for step in (*FAR_FIRST, 0):
                    act(direct(chunk, sibling, 0, step))

    def gathers(level):
        if level == 3:
            return depth != 4
        if level == 4:
            return even
        return depth < 9

    def start(copy):
        copy.start()

    def each_ring(level, chunk, act):
        if level < 3:
            for copy in ring_copies(level, chunk):
                act(copy)
        else:
            @pl.when(gathers(level))
            def _():
                for copy in ring_copies(level, chunk):
                    act(copy)

    def spread(level, chunk):
        each_hop(level, chunk, start)
        each_ring(level, chunk, start)

    def wait_ring(level, chunk):
        for copy in ring_copies(level, chunk):
            copy.wait_recv()

    def set_reduced(slot, chunk, offset):
        span_rows = pl.ds(ROWS * chunk, ROWS)
        value = rhs[slot, span_rows]
        if offset is not None:
            value = value - offset
        rounded = value.astype(BF16)
        red[slot, chunk, 2 * row] = rounded[:, :128]
        red[slot, chunk, 2 * row + 1] = rounded[:, 128:]
        for copy in red_copies(slot, chunk):
            copy.start()

    def offset_of(slot, chunk, limit):
        picked = jnp.concatenate(
            [anc[chunk][jnp.clip(block_rows[slot, r], 0, limit)] for r in range(16)], axis=1
        )
        return jnp.dot(picked, low[slot].reshape(2048, 256), preferred_element_type=F32)

    def solve(slot, chunk):
        for copy in red_copies(slot, chunk):
            copy.wait_recv()
        full = jnp.concatenate([red[slot, chunk, b] for b in range(16)], axis=1)
        solved = jnp.dot(full, inv[slot], preferred_element_type=F32)
        result[slot, pl.ds(ROWS * chunk, ROWS)] = solved
        return solved

    def wait_weights(slot):
        loads[slot, 1].wait()
        halves[slot].wait_recv()

    loads[1, 0].wait()

    @pl.when(depth != 0)
    def _():
        block_rows_copy.wait()

    for level in range(LEVELS):
        @pl.when(depth != level)
        def _():
            if level == 0:
                halves[1].start()
                halves[0].start()
                wait_ready()
            for chunk in range(CHUNKS):
                hop(level, chunk, leaf, 0).wait_recv()
                spread(level, chunk)

        @pl.when(depth == level)
        def _():
            if level > 0:
                loads[1, 2].wait()
            for chunk in range(CHUNKS):
                for above in range(level):
                    wait_ring(above, chunk)
                set_reduced(1, chunk, offset_of(1, chunk, 16 * level - 1) if level else None)
            if level == 0:
                halves[1].start()
            wait_weights(1)
            for chunk in range(CHUNKS):
                rounded = solve(1, chunk).astype(BF16)
                anc[chunk][16 * level + 2 * row] = rounded[:, :128]
                anc[chunk][16 * level + 2 * row + 1] = rounded[:, 128:]
                if level == 0 and chunk == 0:
                    wait_ready()
                spread(level, chunk)
            if level == 0:
                halves[0].start()
                loads[1, 2].wait()
                block_rows_copy.wait()

    @pl.when(depth < 0)
    def _():
        wait_weights(1)
        loads[1, 2].wait()
        result[1] = jnp.zeros_like(result[1])

    upper_out = pltpu.make_async_copy(result.at[1], out.at[1], out_sem.at[1])
    upper_out.start()

    loads[0, 0].wait()
    loads[0, 2].wait()
    wait_weights(0)
    for chunk in range(CHUNKS):
        for level in range(LEVELS):
            @pl.when(depth <= level)
            def _():
                wait_ring(level, chunk)

        set_reduced(0, chunk, offset_of(0, chunk, 79))
    for chunk in range(CHUNKS):
        solve(0, chunk)
    lower_out = pltpu.make_async_copy(result.at[0], out.at[0], out_sem.at[0])
    lower_out.start()

    halves[1].wait_send()
    halves[0].wait_send()

    def wait_send(copy):
        copy.wait_send()

    for chunk in range(CHUNKS):
        for level in range(LEVELS):
            each_hop(level, chunk, wait_send)
            each_ring(level, chunk, wait_send)
        for copy in red_copies(0, chunk):
            copy.wait_send()

        @pl.when(has_upper)
        def _():
            for copy in red_copies(1, chunk):
                copy.wait_send()

    upper_out.wait()
    lower_out.wait()


def local(right_side, inverse_diag, lower_blocks, block_rows):
    anywhere = pl.BlockSpec(memory_space=pl.ANY)
    dma = pltpu.SemaphoreType.DMA
    return pl.pallas_call(
        kernel,
        name="sweep",
        out_shape=jax.ShapeDtypeStruct((2, 64, 256), F32),
        in_specs=[anywhere] * 4,
        out_specs=anywhere,
        scratch_shapes=[
            pltpu.SMEM((2, 16), jnp.int32),
            pltpu.VMEM((2, 64, 256), F32),
            pltpu.VMEM((2, 2048, 256), BF16),
            pltpu.VMEM((2, 16, 128, 256), BF16),
            pltpu.VMEM((80, ROWS, 128), BF16),
            pltpu.VMEM((80, ROWS, 128), BF16),
            pltpu.VMEM((2, CHUNKS, 16, ROWS, 128), BF16),
            pltpu.VMEM((2, 64, 256), F32),
            dma((2, 3)),
            dma((2,)),
            dma((2,)),
            dma((2, CHUNKS, 8)),
            dma((2, CHUNKS, 8)),
            dma((LEVELS, CHUNKS, 2)),
            dma((LEVELS, CHUNKS)),
            dma((LEVELS, CHUNKS, 8)),
            dma((LEVELS, CHUNKS, 8)),
            dma((CHUNKS, 2, 8)),
            dma((2,)),
            dma((1,)),
            pltpu.SemaphoreType.REGULAR,
        ],
        compiler_params=pltpu.CompilerParams(
            collective_id=0, has_side_effects=True, vmem_limit_bytes=56 * 2**20
        ),
    )(block_rows, right_side, inverse_diag, lower_blocks)


def solution(mesh):
    return jax.shard_map(
        local,
        mesh=mesh,
        in_specs=(
            P("leaf", "rhs", "rows"),
            P("leaf", None, ("rows", "rhs")),
            P("leaf", None, None, "rows"),
            P("leaf", None),
        ),
        out_specs=P("leaf", "rhs", "rows"),
        check_vma=False,
    )
```

```python
import jax
import jax.numpy as jnp
from jax import lax
from jax.experimental import pallas as pl
from jax.experimental.pallas import tpu as pltpu
from jax.sharding import PartitionSpec as P

MESH = pl.DeviceIdType.MESH
BF16 = jnp.bfloat16
F32 = jnp.float32
RING = 8
LEVELS = 5
CHUNKS = 4
ROWS = 16
FAR_FIRST = (4, 3, 5, 2, 6, 1, 7)
FAR_UPPER = ()
FAR_LAST = ()
FAR_SIBLING = ()


def device(leaf, row, core):
    return {"leaf": leaf, "rows": row, "rhs": core}


def remote(source, target, sent, arrived, where):
    return pltpu.make_async_remote_copy(
        source, target, sent, arrived, device_id=where, device_id_type=MESH
    )


def depth_of(leaf):
    trail = jnp.int32(0)
    for power in range(1, 6):
        trail = trail + ((leaf + 1) % 2**power == 0).astype(jnp.int32)
    return 4 - trail


def kernel(
    block_rows_in, right_side, inverse_diag, lower_blocks, result,
    block_rows, rhs, inv, low, anc_0, anc_1, anc_2, anc_3, red,
    load_sem, half_send, half_recv, red_send, red_recv, hop_send, hop_recv,
    ring_send, ring_recv, rows_sem, ready,
):
    anc = (anc_0, anc_1, anc_2, anc_3,)
    leaf = lax.axis_index("leaf")
    row = lax.axis_index("rows")
    core = lax.axis_index("rhs")
    even = leaf % 2 == 0
    depth = depth_of(leaf)
    half_span = jnp.int32(0)
    for level in range(4):
        half_span = half_span + jnp.where(depth == level, 2 ** (3 - level), 0)
    span = jnp.maximum(2 * half_span, 1)
    parent = jnp.where((leaf // (2 * span)) % 2 == 0, leaf + span, leaf - span)
    child_a = leaf - half_span
    child_b = leaf + half_span
    has_upper = depth >= 0
    below_root = depth >= 1
    splits = jnp.logical_and(has_upper, depth <= 3)
    sibling = jnp.where(even, leaf + 1, leaf - 1)
    sibling_depth = depth_of(sibling)
    mine_cols = pl.ds(pl.multiple_of(core * 128, 128), 128)

    barrier = pltpu.get_barrier_semaphore()

    def greet(where):
        pl.semaphore_signal(barrier, inc=1, device_id=where, device_id_type=MESH)

    def report(where):
        pl.semaphore_signal(ready, inc=1, device_id=where, device_id_type=MESH)

    for step in FAR_FIRST:
        greet(device(leaf, (row + step) % RING, core))
    greet(device(leaf, row, 1 - core))

    for is_last, far in ((True, FAR_LAST), (False, FAR_UPPER)):
        @pl.when(depth == 3 if is_last else jnp.logical_and(has_upper, depth <= 2))
        def _():
            for step in (*far, 0):
                greet(device(child_a, (row + step) % RING, core))
                greet(device(child_b, (row + step) % RING, core))

    @pl.when(even)
    def _():
        for step in (*FAR_SIBLING, 0):
            greet(device(sibling, (row + step) % RING, core))

    block_rows_copy = pltpu.make_async_copy(block_rows_in, block_rows, rows_sem.at[0])
    loads = {}
    for slot in (1, 0):
        loads[slot, 0] = pltpu.make_async_copy(right_side.at[slot], rhs.at[slot], load_sem.at[slot, 0])
        loads[slot, 1] = pltpu.make_async_copy(
            inverse_diag.at[slot], inv.at[slot, :, mine_cols], load_sem.at[slot, 1]
        )
        loads[slot, 2] = pltpu.make_async_copy(lower_blocks.at[slot], low.at[slot], load_sem.at[slot, 2])
    for copy in loads.values():
        copy.start()
    block_rows_copy.start()

    upper_hops, last_hops, sibling_hops = 1 + len(FAR_UPPER), 1 + len(FAR_LAST), 1 + len(FAR_SIBLING)
    from_parent = jnp.where(depth == 4, last_hops, jnp.where(below_root, upper_hops, 0))
    pl.semaphore_wait(barrier, 8 + from_parent + jnp.where(even, 0, sibling_hops))

    for is_last, far in ((True, FAR_LAST), (False, FAR_UPPER)):
        @pl.when(depth == 4 if is_last else jnp.logical_and(below_root, depth <= 3))
        def _():
            for step in (*far, 0):
                report(device(parent, (row + step) % RING, core))

    @pl.when(jnp.logical_not(even))
    def _():
        for step in (*FAR_SIBLING, 0):
            report(device(sibling, (row + step) % RING, core))

    def wait_ready():
        @pl.when(has_upper)
        def _():
            pl.semaphore_wait(
                ready,
                jnp.where(even, sibling_hops, jnp.where(depth == 3, 2 * last_hops, 2 * upper_hops)),
            )

    halves = {
        slot: remote(
            inverse_diag.at[slot], inv.at[slot, :, mine_cols], half_send.at[slot], half_recv.at[slot],
            device(leaf, row, 1 - core),
        )
        for slot in (1, 0)
    }

    def ring_copies(level, chunk, skipped=()):
        piece = anc[chunk].at[pl.ds(16 * level + 2 * row, 2)]
        return [
            remote(
                piece, piece, ring_send.at[level, chunk, step], ring_recv.at[level, chunk, step],
                device(leaf, (row + step) % RING, core),
            )
            for step in FAR_FIRST
            if step not in skipped
        ]

    def red_copies(slot, chunk):
        piece = red.at[slot, chunk, pl.ds(2 * row, 2)]
        return [
            remote(
                piece, piece, red_send.at[slot, chunk, step], red_recv.at[slot, chunk, step],
                device(leaf, (row + step) % RING, core),
            )
            for step in FAR_FIRST
        ]

    def hop(level, chunk, where, which, step=0):
        piece = anc[chunk].at[pl.ds(16 * level + 2 * row, 2)]
        arrived = ring_recv.at[level, chunk, step] if step else hop_recv.at[level, chunk]
        return remote(
            piece, piece, hop_send.at[level, chunk, which, step], arrived,
            device(where, (row + step) % RING, core),
        )

    def each_hop(level, chunk, act):
        for is_last, far in ((True, FAR_LAST), (False, FAR_UPPER)):
            if level > (3 if is_last else 2):
                continue

            @pl.when(depth == 3 if is_last else jnp.logical_and(depth >= level, depth <= 2))
            def _():
                for step in (0, *far):
                    act(hop(level, chunk, child_a, 0, step))
                    act(hop(level, chunk, child_b, 1, step))

        @pl.when(jnp.logical_and(even, sibling_depth < level))
        def _():
            for step in (0, *FAR_SIBLING):
                act(hop(level, chunk, sibling, 0, step))

    def start(copy):
        copy.start()

    def each_ring(level, chunk, act):
        def run(skipped):
            for copy in ring_copies(level, chunk, skipped):
                act(copy)

        if not (FAR_UPPER or FAR_LAST or FAR_SIBLING):
            run(())
            return

        @pl.when(depth == level)
        def _():
            run(())

        @pl.when(depth < level)
        def _():
            run(FAR_SIBLING)

        if level < 4:
            @pl.when(depth == 4)
            def _():
                run(FAR_LAST)

        if level < 3:
            @pl.when(jnp.logical_and(depth > level, depth < 4))
            def _():
                run(FAR_UPPER)

    def spread(level, chunk):
        each_hop(level, chunk, start)
        each_ring(level, chunk, start)

    def wait_ring(level, chunk):
        for copy in ring_copies(level, chunk):
            copy.wait_recv()

    def set_reduced(slot, chunk, offset):
        span_rows = pl.ds(ROWS * chunk, ROWS)
        value = rhs[slot, span_rows]
        if offset is not None:
            value = value - offset
        rounded = value.astype(BF16)
        red[slot, chunk, 2 * row] = rounded[:, :128]
        red[slot, chunk, 2 * row + 1] = rounded[:, 128:]
        for copy in red_copies(slot, chunk):
            copy.start()

    def offset_of(slot, chunk, limit):
        picked = jnp.concatenate(
            [anc[chunk][jnp.clip(block_rows[slot, r], 0, limit)] for r in range(16)], axis=1
        )
        return jnp.dot(picked, low[slot].reshape(2048, 256), preferred_element_type=F32)

    def solve(slot, chunk):
        for copy in red_copies(slot, chunk):
            copy.wait_recv()
        full = jnp.concatenate([red[slot, chunk, b] for b in range(16)], axis=1)
        solved = jnp.dot(full, inv[slot], preferred_element_type=F32)
        result[slot, pl.ds(ROWS * chunk, ROWS)] = solved
        return solved

    def wait_weights(slot):
        loads[slot, 1].wait()
        halves[slot].wait_recv()

    loads[1, 0].wait()

    @pl.when(depth != 0)
    def _():
        block_rows_copy.wait()

    for level in range(LEVELS):
        @pl.when(depth != level)
        def _():
            if level == 0:
                halves[1].start()
                halves[0].start()
                wait_ready()
            for chunk in range(CHUNKS):
                hop(level, chunk, leaf, 0).wait_recv()
                spread(level, chunk)

        @pl.when(depth == level)
        def _():
            if level > 0:
                loads[1, 2].wait()
            for chunk in range(CHUNKS):
                for above in range(level):
                    wait_ring(above, chunk)
                set_reduced(1, chunk, offset_of(1, chunk, 16 * level - 1) if level else None)
            if level == 0:
                halves[1].start()
            wait_weights(1)
            for chunk in range(CHUNKS):
                rounded = solve(1, chunk).astype(BF16)
                anc[chunk][16 * level + 2 * row] = rounded[:, :128]
                anc[chunk][16 * level + 2 * row + 1] = rounded[:, 128:]
                if level == 0 and chunk == 0:
                    wait_ready()
                spread(level, chunk)
            if level == 0:
                halves[0].start()
                loads[1, 2].wait()
                block_rows_copy.wait()

    @pl.when(depth < 0)
    def _():
        wait_weights(1)
        loads[1, 2].wait()
        result[1] = jnp.zeros_like(result[1])

    loads[0, 0].wait()
    loads[0, 2].wait()
    wait_weights(0)
    for chunk in range(CHUNKS):
        for level in range(LEVELS):
            @pl.when(depth <= level)
            def _():
                wait_ring(level, chunk)

        set_reduced(0, chunk, offset_of(0, chunk, 79))
    for chunk in range(CHUNKS):
        solve(0, chunk)

    halves[1].wait_send()
    halves[0].wait_send()

    def wait_send(copy):
        copy.wait_send()

    for chunk in range(CHUNKS):
        for level in range(LEVELS):
            each_hop(level, chunk, wait_send)
            each_ring(level, chunk, wait_send)
        for copy in red_copies(0, chunk):
            copy.wait_send()

        @pl.when(has_upper)
        def _():
            for copy in red_copies(1, chunk):
                copy.wait_send()


def local(right_side, inverse_diag, lower_blocks, block_rows):
    anywhere = pl.BlockSpec(memory_space=pl.ANY)
    dma = pltpu.SemaphoreType.DMA
    return pl.pallas_call(
        kernel,
        name="sweep",
        out_shape=pltpu.VMEM((2, 64, 256), F32),
        in_specs=[anywhere] * 4,
        out_specs=pl.BlockSpec(memory_space=pltpu.VMEM),
        scratch_shapes=[
            pltpu.SMEM((2, 16), jnp.int32),
            pltpu.VMEM((2, 64, 256), F32),
            pltpu.VMEM((2, 2048, 256), BF16),
            pltpu.VMEM((2, 16, 128, 256), BF16),
            pltpu.VMEM((80, ROWS, 128), BF16),
            pltpu.VMEM((80, ROWS, 128), BF16),
            pltpu.VMEM((80, ROWS, 128), BF16),
            pltpu.VMEM((80, ROWS, 128), BF16),
            pltpu.VMEM((2, CHUNKS, 16, ROWS, 128), BF16),
            dma((2, 3)),
            dma((2,)),
            dma((2,)),
            dma((2, CHUNKS, 8)),
            dma((2, CHUNKS, 8)),
            dma((LEVELS, CHUNKS, 2, 8)),
            dma((LEVELS, CHUNKS)),
            dma((LEVELS, CHUNKS, 8)),
            dma((LEVELS, CHUNKS, 8)),
            dma((1,)),
            pltpu.SemaphoreType.REGULAR,
        ],
        compiler_params=pltpu.CompilerParams(
            collective_id=0, has_side_effects=True, vmem_limit_bytes=56 * 2**20
        ),
    )(block_rows, right_side, inverse_diag, lower_blocks)


def solution(mesh):
    return jax.shard_map(
        local,
        mesh=mesh,
        in_specs=(
            P("leaf", "rhs", "rows"),
            P("leaf", None, ("rows", "rhs")),
            P("leaf", None, None, "rows"),
            P("leaf", None),
        ),
        out_specs=P("leaf", "rhs", "rows"),
        check_vma=False,
    )
```

```python
import jax
import jax.numpy as jnp
from jax import lax
from jax.experimental import pallas as pl
from jax.experimental.pallas import tpu as pltpu
from jax.sharding import PartitionSpec as P

MESH = pl.DeviceIdType.MESH
BF16 = jnp.bfloat16
F32 = jnp.float32
RING = 8
LEVELS = 5
CHUNKS = 4
ROWS = 16
FAR_FIRST = (4, 3, 5, 2, 6, 1, 7)
OTHERS = 2 * len(FAR_FIRST)


def device(leaf, row, core):
    return {"leaf": leaf, "rows": row, "rhs": core}


def remote(source, target, sent, arrived, where):
    return pltpu.make_async_remote_copy(
        source, target, sent, arrived, device_id=where, device_id_type=MESH
    )


def depth_of(leaf):
    trail = jnp.int32(0)
    for power in range(1, 6):
        trail = trail + ((leaf + 1) % 2**power == 0).astype(jnp.int32)
    return 4 - trail


def kernel(
    block_rows_in, right_side, inverse_diag, lower_blocks, result,
    block_rows, rhs, inv, low, anc_0, anc_1, anc_2, anc_3, red,
    load_sem, half_send, half_recv, red_send, red_recv, hop_send, hop_recv,
    ring_send, ring_recv, rows_sem, ready,
):
    anc = (anc_0, anc_1, anc_2, anc_3,)
    leaf = lax.axis_index("leaf")
    row = lax.axis_index("rows")
    core = lax.axis_index("rhs")
    even = leaf % 2 == 0
    depth = depth_of(leaf)
    half_span = jnp.int32(0)
    for level in range(4):
        half_span = half_span + jnp.where(depth == level, 2 ** (3 - level), 0)
    span = jnp.maximum(2 * half_span, 1)
    parent = jnp.where((leaf // (2 * span)) % 2 == 0, leaf + span, leaf - span)
    child_a = leaf - half_span
    child_b = leaf + half_span
    has_upper = depth >= 0
    below_root = depth >= 1
    splits = jnp.logical_and(has_upper, depth <= 3)
    sibling = jnp.where(even, leaf + 1, leaf - 1)
    sibling_depth = depth_of(sibling)
    mine_cols = pl.ds(pl.multiple_of(core * 128, 128), 128)

    barrier = pltpu.get_barrier_semaphore()

    def greet(where):
        pl.semaphore_signal(barrier, inc=1, device_id=where, device_id_type=MESH)

    def report(where):
        pl.semaphore_signal(ready, inc=1, device_id=where, device_id_type=MESH)

    for step in FAR_FIRST:
        greet(device(leaf, (row + step) % RING, core))
    greet(device(leaf, row, 1 - core))

    @pl.when(splits)
    def _():
        greet(device(child_a, row, core))
        greet(device(child_b, row, core))

    @pl.when(even)
    def _():
        greet(device(sibling, row, core))

    block_rows_copy = pltpu.make_async_copy(block_rows_in, block_rows, rows_sem.at[0])
    loads = {}
    for slot in (1, 0):
        loads[slot, 0] = pltpu.make_async_copy(right_side.at[slot], rhs.at[slot], load_sem.at[slot, 0])
        loads[slot, 1] = pltpu.make_async_copy(
            inverse_diag.at[slot], inv.at[slot, :, mine_cols], load_sem.at[slot, 1]
        )
        loads[slot, 2] = pltpu.make_async_copy(lower_blocks.at[slot], low.at[slot], load_sem.at[slot, 2])
    for copy in loads.values():
        copy.start()
    block_rows_copy.start()

    pl.semaphore_wait(barrier, 8 + below_root.astype(jnp.int32) + jnp.where(even, 0, 1))

    @pl.when(below_root)
    def _():
        report(device(parent, row, core))

    @pl.when(jnp.logical_not(even))
    def _():
        report(device(sibling, row, core))

    def wait_ready():
        @pl.when(has_upper)
        def _():
            pl.semaphore_wait(ready, jnp.where(even, 1, 2))

    halves = {
        slot: remote(
            inverse_diag.at[slot], inv.at[slot, :, mine_cols], half_send.at[slot], half_recv.at[slot],
            device(leaf, row, 1 - core),
        )
        for slot in (1, 0)
    }

    def ring_copies(level, chunk):
        piece = anc[chunk].at[pl.ds(16 * level + 2 * row, 2)]
        return [
            remote(
                piece, piece, ring_send.at[chunk], ring_recv.at[level, chunk],
                device(leaf, (row + step) % RING, core),
            )
            for step in FAR_FIRST
        ]

    def red_copies(slot, chunk):
        piece = red.at[slot, chunk, pl.ds(2 * row, 2)]
        return [
            remote(
                piece, piece, red_send.at[slot], red_recv.at[slot, chunk],
                device(leaf, (row + step) % RING, core),
            )
            for step in FAR_FIRST
        ]

    def whole(chunk, blocks, sent, arrived):
        part = anc[chunk].at[pl.ds(0, blocks)]
        return remote(part, part, sent, arrived, device(leaf, row, 1 - core))

    def wait_ring(level, chunk):
        whole(chunk, OTHERS, ring_send.at[chunk], ring_recv.at[level, chunk]).wait_recv()

    def wait_red(slot, chunk):
        whole(chunk, OTHERS, red_send.at[slot], red_recv.at[slot, chunk]).wait_recv()

    def hop(level, chunk, where, which):
        piece = anc[chunk].at[pl.ds(16 * level + 2 * row, 2)]
        return remote(
            piece, piece, hop_send.at[level, which], hop_recv.at[level, chunk],
            device(where, row, core),
        )

    def each_hop(level, act):
        if level < 4:
            @pl.when(jnp.logical_and(splits, depth >= level))
            def _():
                act(child_a, 0)
                act(child_b, 1)

        @pl.when(jnp.logical_and(even, sibling_depth < level))
        def _():
            act(sibling, 0)

    def spread(level, chunk):
        each_hop(level, lambda where, which: hop(level, chunk, where, which).start())
        for copy in ring_copies(level, chunk):
            copy.start()

    def set_reduced(slot, chunk, offset):
        span_rows = pl.ds(ROWS * chunk, ROWS)
        value = rhs[slot, span_rows]
        if offset is not None:
            value = value - offset
        rounded = value.astype(BF16)
        red[slot, chunk, 2 * row] = rounded[:, :128]
        red[slot, chunk, 2 * row + 1] = rounded[:, 128:]
        for copy in red_copies(slot, chunk):
            copy.start()

    def offset_of(slot, chunk, limit):
        picked = jnp.concatenate(
            [anc[chunk][jnp.clip(block_rows[slot, r], 0, limit)] for r in range(16)], axis=1
        )
        return jnp.dot(picked, low[slot].reshape(2048, 256), preferred_element_type=F32)

    def solve(slot, chunk):
        wait_red(slot, chunk)
        full = jnp.concatenate([red[slot, chunk, b] for b in range(16)], axis=1)
        solved = jnp.dot(full, inv[slot], preferred_element_type=F32)
        result[slot, pl.ds(ROWS * chunk, ROWS)] = solved
        return solved

    def wait_weights(slot):
        loads[slot, 1].wait()
        halves[slot].wait_recv()

    loads[1, 0].wait()

    @pl.when(depth != 0)
    def _():
        block_rows_copy.wait()

    for level in range(LEVELS):
        @pl.when(depth != level)
        def _():
            if level == 0:
                halves[1].start()
                halves[0].start()
                wait_ready()
            for chunk in range(CHUNKS):
                hop(level, chunk, leaf, 0).wait_recv()
                spread(level, chunk)

        @pl.when(depth == level)
        def _():
            if level > 0:
                loads[1, 2].wait()
            for chunk in range(CHUNKS):
                for above in range(level):
                    wait_ring(above, chunk)
                set_reduced(1, chunk, offset_of(1, chunk, 16 * level - 1) if level else None)
            if level == 0:
                halves[1].start()
            wait_weights(1)
            for chunk in range(CHUNKS):
                rounded = solve(1, chunk).astype(BF16)
                anc[chunk][16 * level + 2 * row] = rounded[:, :128]
                anc[chunk][16 * level + 2 * row + 1] = rounded[:, 128:]
                if level == 0 and chunk == 0:
                    wait_ready()
                spread(level, chunk)
            if level == 0:
                halves[0].start()
                loads[1, 2].wait()
                block_rows_copy.wait()

    @pl.when(depth < 0)
    def _():
        wait_weights(1)
        loads[1, 2].wait()
        result[1] = jnp.zeros_like(result[1])

    loads[0, 0].wait()
    loads[0, 2].wait()
    wait_weights(0)
    for chunk in range(CHUNKS):
        for level in range(LEVELS):
            @pl.when(depth <= level)
            def _():
                wait_ring(level, chunk)

        set_reduced(0, chunk, offset_of(0, chunk, 79))
    for chunk in range(CHUNKS):
        solve(0, chunk)

    halves[1].wait_send()
    halves[0].wait_send()

    for level in range(LEVELS):
        each_hop(
            level,
            lambda where, which: whole(
                0, 2 * CHUNKS, hop_send.at[level, which], hop_recv.at[level, 0]
            ).wait_send(),
        )
    for chunk in range(CHUNKS):
        whole(chunk, LEVELS * OTHERS, ring_send.at[chunk], ring_recv.at[0, chunk]).wait_send()
    whole(0, CHUNKS * OTHERS, red_send.at[0], red_recv.at[0, 0]).wait_send()

    @pl.when(has_upper)
    def _():
        whole(0, CHUNKS * OTHERS, red_send.at[1], red_recv.at[1, 0]).wait_send()


def local(right_side, inverse_diag, lower_blocks, block_rows):
    anywhere = pl.BlockSpec(memory_space=pl.ANY)
    dma = pltpu.SemaphoreType.DMA
    return pl.pallas_call(
        kernel,
        name="sweep",
        out_shape=pltpu.VMEM((2, 64, 256), F32),
        in_specs=[anywhere] * 4,
        out_specs=pl.BlockSpec(memory_space=pltpu.VMEM),
        scratch_shapes=[
            pltpu.SMEM((2, 16), jnp.int32),
            pltpu.VMEM((2, 64, 256), F32),
            pltpu.VMEM((2, 2048, 256), BF16),
            pltpu.VMEM((2, 16, 128, 256), BF16),
            pltpu.VMEM((80, ROWS, 128), BF16),
            pltpu.VMEM((80, ROWS, 128), BF16),
            pltpu.VMEM((80, ROWS, 128), BF16),
            pltpu.VMEM((80, ROWS, 128), BF16),
            pltpu.VMEM((2, CHUNKS, 16, ROWS, 128), BF16),
            dma((2, 3)),
            dma((2,)),
            dma((2,)),
            dma((2,)),
            dma((2, CHUNKS)),
            dma((LEVELS, 2)),
            dma((LEVELS, CHUNKS)),
            dma((CHUNKS,)),
            dma((LEVELS, CHUNKS)),
            dma((1,)),
            pltpu.SemaphoreType.REGULAR,
        ],
        compiler_params=pltpu.CompilerParams(
            collective_id=0, has_side_effects=True, vmem_limit_bytes=56 * 2**20
        ),
    )(block_rows, right_side, inverse_diag, lower_blocks)


def solution(mesh):
    return jax.shard_map(
        local,
        mesh=mesh,
        in_specs=(
            P("leaf", "rhs", "rows"),
            P("leaf", None, ("rows", "rhs")),
            P("leaf", None, None, "rows"),
            P("leaf", None),
        ),
        out_specs=P("leaf", "rhs", "rows"),
        check_vma=False,
    )
```

```python
import jax
import jax.numpy as jnp
from jax import lax
from jax.experimental import pallas as pl
from jax.experimental.pallas import tpu as pltpu
from jax.sharding import PartitionSpec as P

MESH = pl.DeviceIdType.MESH
BF16 = jnp.bfloat16
F32 = jnp.float32
RING = 8
LEVELS = 5
CHUNKS = 4
ROWS = 16
FAR_FIRST = (4, 3, 5, 2, 6, 1, 7)
OTHERS = 2 * len(FAR_FIRST)


def device(leaf, row, core):
    return {"leaf": leaf, "rows": row, "rhs": core}


def remote(source, target, sent, arrived, where):
    return pltpu.make_async_remote_copy(
        source, target, sent, arrived, device_id=where, device_id_type=MESH
    )


def depth_of(leaf):
    trail = jnp.int32(0)
    for power in range(1, 6):
        trail = trail + ((leaf + 1) % 2**power == 0).astype(jnp.int32)
    return 4 - trail


def kernel(
    block_rows_in, right_side, inverse_diag, lower_blocks, result,
    block_rows, rhs, inv, low, anc_0, anc_1, anc_2, anc_3, last, red, full, fused, total,
    load_sem, half_send, half_recv, red_send, red_recv, hop_send, hop_recv,
    ring_send, ring_recv, rows_sem, pass_send, turn_send, turn_recv, across_send, across_recv, ready,
):
    anc = (anc_0, anc_1, anc_2, anc_3,)
    leaf = lax.axis_index("leaf")
    row = lax.axis_index("rows")
    core = lax.axis_index("rhs")
    even = leaf % 2 == 0
    depth = depth_of(leaf)
    half_span = jnp.int32(0)
    for level in range(4):
        half_span = half_span + jnp.where(depth == level, 2 ** (3 - level), 0)
    span = jnp.maximum(2 * half_span, 1)
    parent = jnp.where((leaf // (2 * span)) % 2 == 0, leaf + span, leaf - span)
    child_a = leaf - half_span
    child_b = leaf + half_span
    has_upper = depth >= 0
    below_root = depth >= 1
    splits = jnp.logical_and(has_upper, depth <= 3)
    sibling = jnp.where(even, leaf + 1, leaf - 1)
    sibling_depth = depth_of(sibling)
    mine_cols = pl.ds(pl.multiple_of(core * 128, 128), 128)

    barrier = pltpu.get_barrier_semaphore()

    def greet(where):
        pl.semaphore_signal(barrier, inc=1, device_id=where, device_id_type=MESH)

    def report(where):
        pl.semaphore_signal(ready, inc=1, device_id=where, device_id_type=MESH)

    for step in FAR_FIRST:
        greet(device(leaf, (row + step) % RING, core))
    greet(device(leaf, row, 1 - core))

    @pl.when(splits)
    def _():
        greet(device(child_a, row, core))
        greet(device(child_b, row, core))

    @pl.when(even)
    def _():
        greet(device(sibling, row, core))

    block_rows_copy = pltpu.make_async_copy(block_rows_in, block_rows, rows_sem.at[0])
    loads = {}
    for slot in (1, 0):
        loads[slot, 0] = pltpu.make_async_copy(right_side.at[slot], rhs.at[slot], load_sem.at[slot, 0])
        loads[slot, 1] = pltpu.make_async_copy(
            inverse_diag.at[slot], inv.at[slot, :, mine_cols], load_sem.at[slot, 1]
        )
        loads[slot, 2] = pltpu.make_async_copy(lower_blocks.at[slot], low.at[slot], load_sem.at[slot, 2])
    for copy in loads.values():
        copy.start()
    block_rows_copy.start()

    pl.semaphore_wait(barrier, 8 + below_root.astype(jnp.int32) + jnp.where(even, 0, 1))

    @pl.when(below_root)
    def _():
        report(device(parent, row, core))

    @pl.when(jnp.logical_not(even))
    def _():
        report(device(sibling, row, core))

    def wait_ready():
        @pl.when(has_upper)
        def _():
            pl.semaphore_wait(ready, jnp.where(even, 1, 2))

    halves = {
        slot: remote(
            inverse_diag.at[slot], inv.at[slot, :, mine_cols], half_send.at[slot], half_recv.at[slot],
            device(leaf, row, 1 - core),
        )
        for slot in (1, 0)
    }

    def piece_at(level, chunk):
        if level == 4:
            return last.at[chunk, pl.ds(2 * row, 2)]
        return anc[chunk].at[pl.ds(16 * level + 2 * row, 2)]

    def ring_copies(level, chunk):
        piece = piece_at(level, chunk)
        return [
            remote(
                piece, piece, ring_send.at[chunk], ring_recv.at[level, chunk],
                device(leaf, (row + step) % RING, core),
            )
            for step in FAR_FIRST
        ]

    def red_copies(slot, chunk):
        piece = red.at[slot, chunk, pl.ds(2 * row, 2)]
        return [
            remote(
                piece, piece, red_send.at[slot], red_recv.at[slot, chunk],
                device(leaf, (row + step) % RING, core),
            )
            for step in FAR_FIRST
        ]

    def whole(chunk, blocks, sent, arrived):
        part = anc[chunk].at[pl.ds(0, blocks)]
        return remote(part, part, sent, arrived, device(leaf, row, 1 - core))

    def wait_ring(level, chunk):
        whole(chunk, OTHERS, ring_send.at[chunk], ring_recv.at[level, chunk]).wait_recv()

    def wait_red(slot, chunk):
        whole(chunk, OTHERS, red_send.at[slot], red_recv.at[slot, chunk]).wait_recv()

    def hop(level, chunk, where, which):
        piece = piece_at(level, chunk)
        return remote(
            piece, piece, hop_send.at[level, which], hop_recv.at[level, chunk],
            device(where, row, core),
        )

    def each_hop(level, act):
        if level < 4:
            @pl.when(jnp.logical_and(depth >= level, depth <= (3 if level >= 2 else 2)))
            def _():
                act(child_a, 0)
                act(child_b, 1)

        @pl.when(jnp.logical_and(even, sibling_depth < level))
        def _():
            act(sibling, 0)

    def spread(level, chunk):
        each_hop(level, lambda where, which: hop(level, chunk, where, which).start())
        for copy in ring_copies(level, chunk):
            copy.start()

    own_half = pl.ds(8 * core, 8)
    quarters = (pl.ds(8 * core, 4), pl.ds(8 * core + 4, 4))

    def turn(step, way, sub):
        piece = (row + RING - way * (step - 1)) % RING
        blocks = quarters[sub]
        source = low.at[1, blocks] if step == 1 else full.at[piece, blocks]
        side = 0 if way == 1 else 1
        return remote(
            source, full.at[piece, blocks], turn_send.at[side], turn_recv.at[step - 1, side, sub],
            device(leaf, (row + RING + way) % RING, core),
        )

    def travels(step, side, sub):
        return step < 4 or side == sub

    def start_turn():
        for sub in range(2):
            for way in (1, -1):
                turn(1, way, sub).start()

    def pass_turn(step):
        for sub in range(2):
            for way, side in ((1, 0), (-1, 1)):
                if not travels(step, side, sub):
                    continue
                piece = (row + RING - way * step) % RING
                turn(step, way, sub).wait_recv()
                if step < 4 and travels(step + 1, side, sub):
                    turn(step + 1, way, sub).start()
                blocks = full.at[piece, quarters[sub]]
                remote(
                    blocks, blocks, across_send.at[0], across_recv.at[step - 1],
                    device(leaf, row, 1 - core),
                ).start()

    def fuse(step):
        if step == 0:
            own_low.wait()
            pieces = [row]
        elif step < 4:
            pieces = [(row + step) % RING, (row + RING - step) % RING]
        else:
            pieces = [(row + step) % RING]
        if step:
            part = full.at[pl.ds(0, len(pieces)), own_half]
            remote(
                part, part, across_send.at[0], across_recv.at[step - 1], device(leaf, row, 1 - core)
            ).wait_recv()

        @pl.loop(0, 8)
        def _(tile):
            rows = pl.ds(pl.multiple_of(256 * tile, 256), 256)
            product = None
            for piece in pieces:
                term = jnp.dot(
                    full[piece, pl.ds(2 * tile, 2)].reshape(256, 256),
                    inv[1, pl.ds(pl.multiple_of(256 * piece, 256), 256)],
                    preferred_element_type=F32,
                )
                product = term if product is None else product + term
            if step:
                product = total[rows, :] + product
            if step < 4:
                total[rows, :] = product
            else:
                fused[rows, :] = product.astype(BF16)

    own_low = pltpu.make_async_copy(lower_blocks.at[1], full.at[row], across_recv.at[4])

    def pass_down(level, chunk, where):
        blocks = anc[chunk].at[pl.ds(16 * level, 16)]
        return remote(
            blocks, blocks, pass_send.at[level], ring_recv.at[level, chunk],
            device(where, row, core),
        )

    def set_reduced(slot, chunk, offset):
        span_rows = pl.ds(ROWS * chunk, ROWS)
        value = rhs[slot, span_rows]
        if offset is not None:
            value = value - offset
        rounded = value.astype(BF16)
        red[slot, chunk, 2 * row] = rounded[:, :128]
        red[slot, chunk, 2 * row + 1] = rounded[:, 128:]
        for copy in red_copies(slot, chunk):
            copy.start()

    def picked_of(slot, chunk, limit):
        return jnp.concatenate(
            [anc[chunk][jnp.clip(block_rows[slot, r], 0, limit)] for r in range(16)], axis=1
        )

    def offset_of(slot, chunk, limit):
        picked = picked_of(slot, chunk, limit)
        return jnp.dot(picked, low[slot].reshape(2048, 256), preferred_element_type=F32)

    def solve(slot, chunk):
        wait_red(slot, chunk)
        full = jnp.concatenate([red[slot, chunk, b] for b in range(16)], axis=1)
        solved = jnp.dot(full, inv[slot], preferred_element_type=F32)
        result[slot, pl.ds(ROWS * chunk, ROWS)] = solved
        return solved

    def wait_weights(slot):
        loads[slot, 1].wait()
        halves[slot].wait_recv()

    loads[1, 0].wait()

    @pl.when(depth != 0)
    def _():
        block_rows_copy.wait()

    @pl.when(depth == 4)
    def _():
        own_low.start()
        halves[1].start()
        for chunk in range(CHUNKS):
            set_reduced(1, chunk, None)
        loads[1, 2].wait()
        start_turn()
        halves[0].start()
        wait_ready()

    @pl.when(jnp.logical_and(depth != 0, depth != 4))
    def _():
        halves[1].start()
        halves[0].start()
        wait_ready()

    for level in range(LEVELS):
        if level < 3:
            @pl.when(depth == 4)
            def _():
                if level == 0:
                    pass_turn(1)
                    wait_weights(1)
                    fuse(0)
                    pass_turn(2)
                    fuse(1)
                elif level == 1:
                    fuse(2)
                    pass_turn(3)
                else:
                    fuse(3)
                    pass_turn(4)
                for chunk in range(CHUNKS):
                    if level < 2:
                        whole(chunk, 16, pass_send.at[level], ring_recv.at[level, chunk]).wait_recv()
                        each_hop(level, lambda where, which: hop(level, chunk, where, which).start())
                    else:
                        hop(level, chunk, leaf, 0).wait_recv()
                        spread(level, chunk)
                if level == 2:
                    fuse(4)
                    for chunk in range(CHUNKS):
                        solve(1, chunk)

            @pl.when(jnp.logical_and(depth != level, depth != 4))
            def _():
                for chunk in range(CHUNKS):
                    hop(level, chunk, leaf, 0).wait_recv()
                    spread(level, chunk)

                if level < 2:
                    @pl.when(depth == 3)
                    def _():
                        for chunk in range(CHUNKS):
                            wait_ring(level, chunk)
                            pass_down(level, chunk, child_a).start()
                            pass_down(level, chunk, child_b).start()
        else:
            @pl.when(depth != level)
            def _():
                for chunk in range(CHUNKS):
                    hop(level, chunk, leaf, 0).wait_recv()
                    spread(level, chunk)

        @pl.when(depth == level)
        def _():
            if level == 4:
                for chunk in range(CHUNKS):
                    wait_ring(2, chunk)
                    wait_ring(3, chunk)
                    rows = pl.ds(ROWS * chunk, ROWS)
                    solved = result[1, rows] - jnp.dot(
                        picked_of(1, chunk, 63), fused[...], preferred_element_type=F32
                    )
                    result[1, rows] = solved
                    rounded = solved.astype(BF16)
                    last[chunk, 2 * row] = rounded[:, :128]
                    last[chunk, 2 * row + 1] = rounded[:, 128:]
                    spread(level, chunk)
                return
            if level > 0:
                loads[1, 2].wait()
            for chunk in range(CHUNKS):
                for above in range(2 if level == 3 else 0, level):
                    wait_ring(above, chunk)
                set_reduced(1, chunk, offset_of(1, chunk, 16 * level - 1) if level else None)
            if level == 0:
                halves[1].start()
            wait_weights(1)
            for chunk in range(CHUNKS):
                rounded = solve(1, chunk).astype(BF16)
                anc[chunk][16 * level + 2 * row] = rounded[:, :128]
                anc[chunk][16 * level + 2 * row + 1] = rounded[:, 128:]
                if level == 0 and chunk == 0:
                    wait_ready()
                spread(level, chunk)
            if level == 0:
                halves[0].start()
                loads[1, 2].wait()
                block_rows_copy.wait()

    @pl.when(depth < 0)
    def _():
        wait_weights(1)
        loads[1, 2].wait()
        result[1] = jnp.zeros_like(result[1])

    loads[0, 0].wait()
    loads[0, 2].wait()
    wait_weights(0)
    for chunk in range(CHUNKS):
        for level in range(LEVELS):
            @pl.when(depth <= level)
            def _():
                wait_ring(level, chunk)

        for block in range(16):
            anc[chunk][64 + block] = last[chunk, block]
        set_reduced(0, chunk, offset_of(0, chunk, 79))
    for chunk in range(CHUNKS):
        solve(0, chunk)

    halves[1].wait_send()
    halves[0].wait_send()

    for level in range(LEVELS):
        each_hop(
            level,
            lambda where, which: whole(
                0, 2 * CHUNKS, hop_send.at[level, which], hop_recv.at[level, 0]
            ).wait_send(),
        )
    for chunk in range(CHUNKS):
        for is_fused, levels in ((True, 3), (False, LEVELS)):
            @pl.when((depth == 4) == is_fused)
            def _():
                whole(chunk, levels * OTHERS, ring_send.at[chunk], ring_recv.at[0, chunk]).wait_send()

    @pl.when(depth == 3)
    def _():
        for level in range(2):
            part = low.at[0, pl.ds(0, 8)]
            remote(
                part, part, pass_send.at[level], ring_recv.at[level, 0], device(child_a, row, core)
            ).wait_send()

    @pl.when(depth == 4)
    def _():
        for side in range(2):
            part = low.at[:, pl.ds(0, 14)]
            remote(
                part, part, turn_send.at[side], turn_recv.at[0, side], device(leaf, row, 1 - core)
            ).wait_send()
        part = full.at[pl.ds(0, 7), own_half]
        remote(
            part, part, across_send.at[0], across_recv.at[0], device(leaf, row, 1 - core)
        ).wait_send()

    whole(0, CHUNKS * OTHERS, red_send.at[0], red_recv.at[0, 0]).wait_send()

    @pl.when(has_upper)
    def _():
        whole(0, CHUNKS * OTHERS, red_send.at[1], red_recv.at[1, 0]).wait_send()


def local(right_side, inverse_diag, lower_blocks, block_rows):
    anywhere = pl.BlockSpec(memory_space=pl.ANY)
    dma = pltpu.SemaphoreType.DMA
    return pl.pallas_call(
        kernel,
        name="sweep",
        out_shape=pltpu.VMEM((2, 64, 256), F32),
        in_specs=[anywhere] * 4,
        out_specs=pl.BlockSpec(memory_space=pltpu.VMEM),
        scratch_shapes=[
            pltpu.SMEM((2, 16), jnp.int32),
            pltpu.VMEM((2, 64, 256), F32),
            pltpu.VMEM((2, 2048, 256), BF16),
            pltpu.VMEM((2, 16, 128, 256), BF16),
            pltpu.VMEM((80, ROWS, 128), BF16),
            pltpu.VMEM((80, ROWS, 128), BF16),
            pltpu.VMEM((80, ROWS, 128), BF16),
            pltpu.VMEM((80, ROWS, 128), BF16),
            pltpu.VMEM((CHUNKS, 16, ROWS, 128), BF16),
            pltpu.VMEM((2, CHUNKS, 16, ROWS, 128), BF16),
            pltpu.VMEM((RING, 16, 128, 256), BF16),
            pltpu.VMEM((2048, 256), BF16),
            pltpu.VMEM((2048, 256), F32),
            dma((2, 3)),
            dma((2,)),
            dma((2,)),
            dma((2,)),
            dma((2, CHUNKS)),
            dma((LEVELS, 2)),
            dma((LEVELS, CHUNKS)),
            dma((CHUNKS,)),
            dma((LEVELS, CHUNKS)),
            dma((1,)),
            dma((2,)),
            dma((2,)),
            dma((4, 2, 2)),
            dma((1,)),
            dma((5,)),
            pltpu.SemaphoreType.REGULAR,
        ],
        compiler_params=pltpu.CompilerParams(
            collective_id=0, has_side_effects=True, vmem_limit_bytes=56 * 2**20
        ),
    )(block_rows, right_side, inverse_diag, lower_blocks)


def solution(mesh):
    return jax.shard_map(
        local,
        mesh=mesh,
        in_specs=(
            P("leaf", "rhs", "rows"),
            P("leaf", None, ("rows", "rhs")),
            P("leaf", None, None, "rows"),
            P("leaf", None),
        ),
        out_specs=P("leaf", "rhs", "rows"),
        check_vma=False,
    )
```

```python
import jax
import jax.numpy as jnp
from jax import lax
from jax.experimental import pallas as pl
from jax.experimental.pallas import tpu as pltpu
from jax.sharding import PartitionSpec as P

MESH = pl.DeviceIdType.MESH
BF16 = jnp.bfloat16
F32 = jnp.float32
RING = 8
LEVELS = 5
CHUNKS = 4
ROWS = 16
FAR_FIRST = (4, 3, 5, 2, 6, 1, 7)
OTHERS = 2 * len(FAR_FIRST)


def device(leaf, row, core):
    return {"leaf": leaf, "rows": row, "rhs": core}


def remote(source, target, sent, arrived, where):
    return pltpu.make_async_remote_copy(
        source, target, sent, arrived, device_id=where, device_id_type=MESH
    )


def depth_of(leaf):
    trail = jnp.int32(0)
    for power in range(1, 6):
        trail = trail + ((leaf + 1) % 2**power == 0).astype(jnp.int32)
    return 4 - trail


def kernel(
    block_rows_in, right_side, inverse_diag, lower_blocks, result,
    block_rows, rhs, inv, low, anc_0, anc_1, anc_2, anc_3, last, red, full, fused, total,
    load_sem, half_send, half_recv, red_send, red_recv, hop_send, hop_recv,
    ring_send, ring_recv, rows_sem, pass_send, turn_send, turn_recv, across_send, across_recv, ready,
):
    anc = (anc_0, anc_1, anc_2, anc_3,)
    leaf = lax.axis_index("leaf")
    row = lax.axis_index("rows")
    core = lax.axis_index("rhs")
    even = leaf % 2 == 0
    depth = depth_of(leaf)
    half_span = jnp.int32(0)
    for level in range(4):
        half_span = half_span + jnp.where(depth == level, 2 ** (3 - level), 0)
    span = jnp.maximum(2 * half_span, 1)
    parent = jnp.where((leaf // (2 * span)) % 2 == 0, leaf + span, leaf - span)
    child_a = leaf - half_span
    child_b = leaf + half_span
    has_upper = depth >= 0
    below_root = depth >= 1
    splits = jnp.logical_and(has_upper, depth <= 3)
    sibling = jnp.where(even, leaf + 1, leaf - 1)
    sibling_depth = depth_of(sibling)
    mine_cols = pl.ds(pl.multiple_of(core * 128, 128), 128)

    barrier = pltpu.get_barrier_semaphore()

    def greet(where):
        pl.semaphore_signal(barrier, inc=1, device_id=where, device_id_type=MESH)

    def report(where):
        pl.semaphore_signal(ready, inc=1, device_id=where, device_id_type=MESH)

    for step in FAR_FIRST:
        greet(device(leaf, (row + step) % RING, core))
    greet(device(leaf, row, 1 - core))

    @pl.when(splits)
    def _():
        greet(device(child_a, row, core))
        greet(device(child_b, row, core))

    @pl.when(even)
    def _():
        greet(device(sibling, row, core))

    block_rows_copy = pltpu.make_async_copy(block_rows_in, block_rows, rows_sem.at[0])
    loads = {}
    for slot in (1, 0):
        loads[slot, 0] = pltpu.make_async_copy(right_side.at[slot], rhs.at[slot], load_sem.at[slot, 0])
        loads[slot, 1] = pltpu.make_async_copy(
            inverse_diag.at[slot], inv.at[slot, :, mine_cols], load_sem.at[slot, 1]
        )
        loads[slot, 2] = pltpu.make_async_copy(lower_blocks.at[slot], low.at[slot], load_sem.at[slot, 2])
    for copy in loads.values():
        copy.start()
    block_rows_copy.start()

    pl.semaphore_wait(barrier, 8 + below_root.astype(jnp.int32) + jnp.where(even, 0, 1))

    @pl.when(below_root)
    def _():
        report(device(parent, row, core))

    @pl.when(jnp.logical_not(even))
    def _():
        report(device(sibling, row, core))

    def wait_ready():
        @pl.when(has_upper)
        def _():
            pl.semaphore_wait(ready, jnp.where(even, 1, 2))

    halves = {
        slot: remote(
            inverse_diag.at[slot], inv.at[slot, :, mine_cols], half_send.at[slot], half_recv.at[slot],
            device(leaf, row, 1 - core),
        )
        for slot in (1, 0)
    }

    def piece_at(level, chunk):
        if level == 4:
            return last.at[chunk, pl.ds(2 * row, 2)]
        return anc[chunk].at[pl.ds(16 * level + 2 * row, 2)]

    def ring_copies(level, chunk):
        piece = piece_at(level, chunk)
        return [
            remote(
                piece, piece, ring_send.at[chunk], ring_recv.at[level, chunk],
                device(leaf, (row + step) % RING, core),
            )
            for step in FAR_FIRST
        ]

    def red_copies(slot, chunk):
        piece = red.at[slot, chunk, pl.ds(2 * row, 2)]
        return [
            remote(
                piece, piece, red_send.at[slot], red_recv.at[slot, chunk],
                device(leaf, (row + step) % RING, core),
            )
            for step in FAR_FIRST
        ]

    def whole(chunk, blocks, sent, arrived):
        part = anc[chunk].at[pl.ds(0, blocks)]
        return remote(part, part, sent, arrived, device(leaf, row, 1 - core))

    def wait_ring(level, chunk):
        whole(chunk, OTHERS, ring_send.at[chunk], ring_recv.at[level, chunk]).wait_recv()

    def wait_red(slot, chunk):
        whole(chunk, OTHERS, red_send.at[slot], red_recv.at[slot, chunk]).wait_recv()

    def hop(level, chunk, where, which):
        piece = piece_at(level, chunk)
        return remote(
            piece, piece, hop_send.at[level, which], hop_recv.at[level, chunk],
            device(where, row, core),
        )

    def each_hop(level, act):
        if level < 4:
            @pl.when(jnp.logical_and(depth >= level, depth <= (3 if level >= 2 else 2)))
            def _():
                act(child_a, 0)
                act(child_b, 1)

        @pl.when(jnp.logical_and(even, sibling_depth < level))
        def _():
            act(sibling, 0)

    def spread(level, chunk):
        each_hop(level, lambda where, which: hop(level, chunk, where, which).start())
        for copy in ring_copies(level, chunk):
            copy.start()

    own_half = pl.ds(8 * core, 8)
    quarters = (pl.ds(8 * core, 4), pl.ds(8 * core + 4, 4))

    def turn(step, way, sub):
        piece = (row + RING - way * (step - 1)) % RING
        blocks = quarters[sub]
        source = low.at[1, blocks] if step == 1 else full.at[piece, blocks]
        side = 0 if way == 1 else 1
        return remote(
            source, full.at[piece, blocks], turn_send.at[side], turn_recv.at[step - 1, side, sub],
            device(leaf, (row + RING + way) % RING, core),
        )

    def travels(step, side, sub):
        return step < 4 or side == sub

    def start_turn():
        for sub in range(2):
            for way in (1, -1):
                turn(1, way, sub).start()

    def pass_turn(step):
        for sub in range(2):
            for way, side in ((1, 0), (-1, 1)):
                if not travels(step, side, sub):
                    continue
                piece = (row + RING - way * step) % RING
                turn(step, way, sub).wait_recv()
                if step < 4 and travels(step + 1, side, sub):
                    turn(step + 1, way, sub).start()
                blocks = full.at[piece, quarters[sub]]
                remote(
                    blocks, blocks, across_send.at[0], across_recv.at[step - 1],
                    device(leaf, row, 1 - core),
                ).start()

    def fuse(step):
        if step == 0:
            own_low.wait()
            pieces = [row]
        elif step < 4:
            pieces = [(row + step) % RING, (row + RING - step) % RING]
        else:
            pieces = [(row + step) % RING]
        if step:
            part = full.at[pl.ds(0, len(pieces)), own_half]
            remote(
                part, part, across_send.at[0], across_recv.at[step - 1], device(leaf, row, 1 - core)
            ).wait_recv()

        @pl.loop(0, 8)
        def _(tile):
            rows = pl.ds(pl.multiple_of(256 * tile, 256), 256)
            product = None
            for piece in pieces:
                term = jnp.dot(
                    full[piece, pl.ds(2 * tile, 2)].reshape(256, 256),
                    inv[1, pl.ds(pl.multiple_of(256 * piece, 256), 256)],
                    preferred_element_type=F32,
                )
                product = term if product is None else product + term
            if step:
                product = total[rows, :] + product
            if step < 4:
                total[rows, :] = product
            else:
                fused[rows, :] = product.astype(BF16)

    own_low = pltpu.make_async_copy(lower_blocks.at[1], full.at[row], across_recv.at[4])

    def pass_down(level, chunk, where):
        blocks = anc[chunk].at[pl.ds(16 * level, 16)]
        return remote(
            blocks, blocks, pass_send.at[level], ring_recv.at[level, chunk],
            device(where, row, core),
        )

    def set_reduced(slot, chunk, offset):
        span_rows = pl.ds(ROWS * chunk, ROWS)
        value = rhs[slot, span_rows]
        if offset is not None:
            value = value - offset
        rounded = value.astype(BF16)
        red[slot, chunk, 2 * row] = rounded[:, :128]
        red[slot, chunk, 2 * row + 1] = rounded[:, 128:]
        for copy in red_copies(slot, chunk):
            copy.start()

    def picked_of(slot, chunk, limit):
        return jnp.concatenate(
            [anc[chunk][jnp.clip(block_rows[slot, r], 0, limit)] for r in range(16)], axis=1
        )

    def offset_of(slot, chunk, limit):
        picked = picked_of(slot, chunk, limit)
        return jnp.dot(picked, low[slot].reshape(2048, 256), preferred_element_type=F32)

    def solve(slot, chunk):
        wait_red(slot, chunk)
        full = jnp.concatenate([red[slot, chunk, b] for b in range(16)], axis=1)
        solved = jnp.dot(full, inv[slot], preferred_element_type=F32)
        result[slot, pl.ds(ROWS * chunk, ROWS)] = solved
        return solved

    def wait_weights(slot):
        loads[slot, 1].wait()
        halves[slot].wait_recv()

    loads[1, 0].wait()

    @pl.when(depth != 0)
    def _():
        block_rows_copy.wait()

    @pl.when(depth == 4)
    def _():
        own_low.start()
        halves[1].start()
        loads[1, 2].wait()
        start_turn()
        for chunk in range(CHUNKS):
            set_reduced(1, chunk, None)
        halves[0].start()
        wait_ready()

    @pl.when(jnp.logical_and(depth != 0, depth != 4))
    def _():
        halves[1].start()
        halves[0].start()
        wait_ready()

    for level in range(LEVELS):
        if level < 3:
            @pl.when(depth == 4)
            def _():
                if level == 0:
                    pass_turn(1)
                    wait_weights(1)
                    fuse(0)
                    pass_turn(2)
                    fuse(1)
                elif level == 1:
                    fuse(2)
                    pass_turn(3)
                else:
                    fuse(3)
                    pass_turn(4)
                for chunk in range(CHUNKS):
                    if level < 2:
                        whole(chunk, 16, pass_send.at[level], ring_recv.at[level, chunk]).wait_recv()
                        each_hop(level, lambda where, which: hop(level, chunk, where, which).start())
                    else:
                        hop(level, chunk, leaf, 0).wait_recv()
                        spread(level, chunk)
                if level == 2:
                    fuse(4)
                    for chunk in range(CHUNKS):
                        solve(1, chunk)

            @pl.when(jnp.logical_and(depth != level, depth != 4))
            def _():
                for chunk in range(CHUNKS):
                    hop(level, chunk, leaf, 0).wait_recv()
                    spread(level, chunk)

                if level < 2:
                    @pl.when(depth == 3)
                    def _():
                        for chunk in range(CHUNKS):
                            wait_ring(level, chunk)
                            pass_down(level, chunk, child_a).start()
                            pass_down(level, chunk, child_b).start()
        else:
            @pl.when(depth != level)
            def _():
                for chunk in range(CHUNKS):
                    hop(level, chunk, leaf, 0).wait_recv()
                    spread(level, chunk)

        @pl.when(depth == level)
        def _():
            if level == 4:
                for chunk in range(CHUNKS):
                    wait_ring(2, chunk)
                    wait_ring(3, chunk)
                    rows = pl.ds(ROWS * chunk, ROWS)
                    solved = result[1, rows] - jnp.dot(
                        picked_of(1, chunk, 63), fused[...], preferred_element_type=F32
                    )
                    result[1, rows] = solved
                    rounded = solved.astype(BF16)
                    last[chunk, 2 * row] = rounded[:, :128]
                    last[chunk, 2 * row + 1] = rounded[:, 128:]
                    spread(level, chunk)
                return
            if level > 0:
                loads[1, 2].wait()
            for chunk in range(CHUNKS):
                for above in range(2 if level == 3 else 0, level):
                    wait_ring(above, chunk)
                set_reduced(1, chunk, offset_of(1, chunk, 16 * level - 1) if level else None)
            if level == 0:
                halves[1].start()
            wait_weights(1)
            for chunk in range(CHUNKS):
                rounded = solve(1, chunk).astype(BF16)
                anc[chunk][16 * level + 2 * row] = rounded[:, :128]
                anc[chunk][16 * level + 2 * row + 1] = rounded[:, 128:]
                if level == 0 and chunk == 0:
                    wait_ready()
                spread(level, chunk)
            if level == 0:
                halves[0].start()
                loads[1, 2].wait()
                block_rows_copy.wait()

    @pl.when(depth < 0)
    def _():
        wait_weights(1)
        loads[1, 2].wait()
        result[1] = jnp.zeros_like(result[1])

    loads[0, 0].wait()
    loads[0, 2].wait()
    wait_weights(0)
    for chunk in range(CHUNKS):
        for level in range(LEVELS):
            @pl.when(depth <= level)
            def _():
                wait_ring(level, chunk)

        for block in range(16):
            anc[chunk][64 + block] = last[chunk, block]
        set_reduced(0, chunk, offset_of(0, chunk, 79))
    for chunk in range(CHUNKS):
        solve(0, chunk)

    halves[1].wait_send()
    halves[0].wait_send()

    for level in range(LEVELS):
        each_hop(
            level,
            lambda where, which: whole(
                0, 2 * CHUNKS, hop_send.at[level, which], hop_recv.at[level, 0]
            ).wait_send(),
        )
    for chunk in range(CHUNKS):
        for is_fused, levels in ((True, 3), (False, LEVELS)):
            @pl.when((depth == 4) == is_fused)
            def _():
                whole(chunk, levels * OTHERS, ring_send.at[chunk], ring_recv.at[0, chunk]).wait_send()

    @pl.when(depth == 3)
    def _():
        for level in range(2):
            part = low.at[0, pl.ds(0, 8)]
            remote(
                part, part, pass_send.at[level], ring_recv.at[level, 0], device(child_a, row, core)
            ).wait_send()

    @pl.when(depth == 4)
    def _():
        for side in range(2):
            part = low.at[:, pl.ds(0, 14)]
            remote(
                part, part, turn_send.at[side], turn_recv.at[0, side], device(leaf, row, 1 - core)
            ).wait_send()
        part = full.at[pl.ds(0, 7), own_half]
        remote(
            part, part, across_send.at[0], across_recv.at[0], device(leaf, row, 1 - core)
        ).wait_send()

    whole(0, CHUNKS * OTHERS, red_send.at[0], red_recv.at[0, 0]).wait_send()

    @pl.when(has_upper)
    def _():
        whole(0, CHUNKS * OTHERS, red_send.at[1], red_recv.at[1, 0]).wait_send()


def local(right_side, inverse_diag, lower_blocks, block_rows):
    anywhere = pl.BlockSpec(memory_space=pl.ANY)
    dma = pltpu.SemaphoreType.DMA
    return pl.pallas_call(
        kernel,
        name="sweep",
        out_shape=pltpu.VMEM((2, 64, 256), F32),
        in_specs=[anywhere] * 4,
        out_specs=pl.BlockSpec(memory_space=pltpu.VMEM),
        scratch_shapes=[
            pltpu.SMEM((2, 16), jnp.int32),
            pltpu.VMEM((2, 64, 256), F32),
            pltpu.VMEM((2, 2048, 256), BF16),
            pltpu.VMEM((2, 16, 128, 256), BF16),
            pltpu.VMEM((80, ROWS, 128), BF16),
            pltpu.VMEM((80, ROWS, 128), BF16),
            pltpu.VMEM((80, ROWS, 128), BF16),
            pltpu.VMEM((80, ROWS, 128), BF16),
            pltpu.VMEM((CHUNKS, 16, ROWS, 128), BF16),
            pltpu.VMEM((2, CHUNKS, 16, ROWS, 128), BF16),
            pltpu.VMEM((RING, 16, 128, 256), BF16),
            pltpu.VMEM((2048, 256), BF16),
            pltpu.VMEM((2048, 256), F32),
            dma((2, 3)),
            dma((2,)),
            dma((2,)),
            dma((2,)),
            dma((2, CHUNKS)),
            dma((LEVELS, 2)),
            dma((LEVELS, CHUNKS)),
            dma((CHUNKS,)),
            dma((LEVELS, CHUNKS)),
            dma((1,)),
            dma((2,)),
            dma((2,)),
            dma((4, 2, 2)),
            dma((1,)),
            dma((5,)),
            pltpu.SemaphoreType.REGULAR,
        ],
        compiler_params=pltpu.CompilerParams(
            collective_id=0, has_side_effects=True, vmem_limit_bytes=56 * 2**20
        ),
    )(block_rows, right_side, inverse_diag, lower_blocks)


def solution(mesh):
    return jax.shard_map(
        local,
        mesh=mesh,
        in_specs=(
            P("leaf", "rhs", "rows"),
            P("leaf", None, ("rows", "rhs")),
            P("leaf", None, None, "rows"),
            P("leaf", None),
        ),
        out_specs=P("leaf", "rhs", "rows"),
        check_vma=False,
    )
```

```python
import jax
import jax.numpy as jnp
from jax import lax
from jax.experimental import pallas as pl
from jax.experimental.pallas import tpu as pltpu
from jax.sharding import PartitionSpec as P

MESH = pl.DeviceIdType.MESH
BF16 = jnp.bfloat16
F32 = jnp.float32
RING = 8
LEVELS = 5
CHUNKS = 4
ROWS = 16
FAR_FIRST = (4, 3, 5, 2, 6, 1, 7)
OTHERS = 2 * len(FAR_FIRST)


def device(leaf, row, core):
    return {"leaf": leaf, "rows": row, "rhs": core}


def remote(source, target, sent, arrived, where):
    return pltpu.make_async_remote_copy(
        source, target, sent, arrived, device_id=where, device_id_type=MESH
    )


def depth_of(leaf):
    trail = jnp.int32(0)
    for power in range(1, 6):
        trail = trail + ((leaf + 1) % 2**power == 0).astype(jnp.int32)
    return 4 - trail


def kernel(
    block_rows_in, right_side, inverse_diag, lower_blocks, result,
    block_rows, rhs, inv, low, anc_0, anc_1, anc_2, anc_3, last, red, full, fused, total,
    load_sem, half_send, half_recv, red_send, red_recv, hop_send, hop_recv,
    ring_send, ring_recv, rows_sem, pass_send, turn_send, turn_recv, across_send, across_recv, ready,
):
    anc = (anc_0, anc_1, anc_2, anc_3,)
    leaf = lax.axis_index("leaf")
    row = lax.axis_index("rows")
    core = lax.axis_index("rhs")
    even = leaf % 2 == 0
    depth = depth_of(leaf)
    half_span = jnp.int32(0)
    for level in range(4):
        half_span = half_span + jnp.where(depth == level, 2 ** (3 - level), 0)
    span = jnp.maximum(2 * half_span, 1)
    parent = jnp.where((leaf // (2 * span)) % 2 == 0, leaf + span, leaf - span)
    child_a = leaf - half_span
    child_b = leaf + half_span
    has_upper = depth >= 0
    below_root = depth >= 1
    splits = jnp.logical_and(has_upper, depth <= 3)
    sibling = jnp.where(even, leaf + 1, leaf - 1)
    sibling_depth = depth_of(sibling)
    mine_cols = pl.ds(pl.multiple_of(core * 128, 128), 128)

    barrier = pltpu.get_barrier_semaphore()

    def greet(where):
        pl.semaphore_signal(barrier, inc=1, device_id=where, device_id_type=MESH)

    def report(where):
        pl.semaphore_signal(ready, inc=1, device_id=where, device_id_type=MESH)

    for step in FAR_FIRST:
        greet(device(leaf, (row + step) % RING, core))
    greet(device(leaf, row, 1 - core))

    @pl.when(splits)
    def _():
        greet(device(child_a, row, core))
        greet(device(child_b, row, core))

    @pl.when(even)
    def _():
        greet(device(sibling, row, core))

    block_rows_copy = pltpu.make_async_copy(block_rows_in, block_rows, rows_sem.at[0])
    loads = {}
    for slot in (1, 0):
        loads[slot, 0] = pltpu.make_async_copy(right_side.at[slot], rhs.at[slot], load_sem.at[slot, 0])
        loads[slot, 1] = pltpu.make_async_copy(
            inverse_diag.at[slot], inv.at[slot, :, mine_cols], load_sem.at[slot, 1]
        )
        loads[slot, 2] = pltpu.make_async_copy(lower_blocks.at[slot], low.at[slot], load_sem.at[slot, 2])
    for copy in loads.values():
        copy.start()
    block_rows_copy.start()

    pl.semaphore_wait(barrier, 8 + below_root.astype(jnp.int32) + jnp.where(even, 0, 1))

    @pl.when(below_root)
    def _():
        report(device(parent, row, core))

    @pl.when(jnp.logical_not(even))
    def _():
        report(device(sibling, row, core))

    def wait_ready():
        @pl.when(has_upper)
        def _():
            pl.semaphore_wait(ready, jnp.where(even, 1, 2))

    halves = {
        slot: remote(
            inverse_diag.at[slot], inv.at[slot, :, mine_cols], half_send.at[slot], half_recv.at[slot],
            device(leaf, row, 1 - core),
        )
        for slot in (1, 0)
    }

    def piece_at(level, chunk):
        if level == 4:
            return last.at[chunk, pl.ds(2 * row, 2)]
        return anc[chunk].at[pl.ds(16 * level + 2 * row, 2)]

    def ring_copies(level, chunk):
        piece = piece_at(level, chunk)
        return [
            remote(
                piece, piece, ring_send.at[chunk], ring_recv.at[level, chunk],
                device(leaf, (row + step) % RING, core),
            )
            for step in FAR_FIRST
        ]

    def red_copies(slot, chunk):
        piece = red.at[slot, chunk, pl.ds(2 * row, 2)]
        return [
            remote(
                piece, piece, red_send.at[slot], red_recv.at[slot, chunk],
                device(leaf, (row + step) % RING, core),
            )
            for step in FAR_FIRST
        ]

    def whole(chunk, blocks, sent, arrived):
        part = anc[chunk].at[pl.ds(0, blocks)]
        return remote(part, part, sent, arrived, device(leaf, row, 1 - core))

    def wait_ring(level, chunk):
        whole(chunk, OTHERS, ring_send.at[chunk], ring_recv.at[level, chunk]).wait_recv()

    def wait_red(slot, chunk):
        whole(chunk, OTHERS, red_send.at[slot], red_recv.at[slot, chunk]).wait_recv()

    def hop(level, chunk, where, which):
        piece = piece_at(level, chunk)
        return remote(
            piece, piece, hop_send.at[level, which], hop_recv.at[level, chunk],
            device(where, row, core),
        )

    def each_hop(level, act):
        if level < 4:
            @pl.when(jnp.logical_and(depth >= level, depth <= (3 if level >= 2 else 2)))
            def _():
                act(child_a, 0)
                act(child_b, 1)

        @pl.when(jnp.logical_and(even, sibling_depth < level))
        def _():
            act(sibling, 0)

    def start_hops(level, chunk):
        each_hop(level, lambda where, which: hop(level, chunk, where, which).start())

    def start_ring(level, chunk):
        for copy in ring_copies(level, chunk):
            copy.start()

    def spread(level, chunk):
        start_hops(level, chunk)
        start_ring(level, chunk)

    own_half = pl.ds(8 * core, 8)
    quarters = (pl.ds(8 * core, 4), pl.ds(8 * core + 4, 4))

    def turn(step, way, sub):
        piece = (row + RING - way * (step - 1)) % RING
        blocks = quarters[sub]
        source = low.at[1, blocks] if step == 1 else full.at[piece, blocks]
        side = 0 if way == 1 else 1
        return remote(
            source, full.at[piece, blocks], turn_send.at[side], turn_recv.at[step - 1, side, sub],
            device(leaf, (row + RING + way) % RING, core),
        )

    def travels(step, side, sub):
        return step < 4 or side == sub

    def start_turn():
        for sub in range(2):
            for way in (1, -1):
                turn(1, way, sub).start()

    def pass_turn(step):
        for sub in range(2):
            for way, side in ((1, 0), (-1, 1)):
                if not travels(step, side, sub):
                    continue
                piece = (row + RING - way * step) % RING
                turn(step, way, sub).wait_recv()
                if step < 4 and travels(step + 1, side, sub):
                    turn(step + 1, way, sub).start()
                blocks = full.at[piece, quarters[sub]]
                remote(
                    blocks, blocks, across_send.at[0], across_recv.at[step - 1],
                    device(leaf, row, 1 - core),
                ).start()

    def fuse(step):
        if step == 0:
            own_low.wait()
            pieces = [row]
        elif step < 4:
            pieces = [(row + step) % RING, (row + RING - step) % RING]
        else:
            pieces = [(row + step) % RING]
        if step:
            part = full.at[pl.ds(0, len(pieces)), own_half]
            remote(
                part, part, across_send.at[0], across_recv.at[step - 1], device(leaf, row, 1 - core)
            ).wait_recv()

        @pl.loop(0, 8)
        def _(tile):
            rows = pl.ds(pl.multiple_of(256 * tile, 256), 256)
            product = None
            for piece in pieces:
                term = jnp.dot(
                    full[piece, pl.ds(2 * tile, 2)].reshape(256, 256),
                    inv[1, pl.ds(pl.multiple_of(256 * piece, 256), 256)],
                    preferred_element_type=F32,
                )
                product = term if product is None else product + term
            if step:
                product = total[rows, :] + product
            if step < 4:
                total[rows, :] = product
            else:
                fused[rows, :] = product.astype(BF16)

    own_low = pltpu.make_async_copy(lower_blocks.at[1], full.at[row], across_recv.at[4])

    def pass_down(level, chunk, where):
        blocks = anc[chunk].at[pl.ds(16 * level, 16)]
        return remote(
            blocks, blocks, pass_send.at[level], ring_recv.at[level, chunk],
            device(where, row, core),
        )

    def set_reduced(slot, chunk, offset):
        span_rows = pl.ds(ROWS * chunk, ROWS)
        value = rhs[slot, span_rows]
        if offset is not None:
            value = value - offset
        rounded = value.astype(BF16)
        red[slot, chunk, 2 * row] = rounded[:, :128]
        red[slot, chunk, 2 * row + 1] = rounded[:, 128:]
        for copy in red_copies(slot, chunk):
            copy.start()

    def picked_of(slot, chunk, limit):
        return jnp.concatenate(
            [anc[chunk][jnp.clip(block_rows[slot, r], 0, limit)] for r in range(16)], axis=1
        )

    def offset_of(slot, chunk, limit):
        picked = picked_of(slot, chunk, limit)
        return jnp.dot(picked, low[slot].reshape(2048, 256), preferred_element_type=F32)

    def solve(slot, chunk):
        wait_red(slot, chunk)
        full = jnp.concatenate([red[slot, chunk, b] for b in range(16)], axis=1)
        solved = jnp.dot(full, inv[slot], preferred_element_type=F32)
        result[slot, pl.ds(ROWS * chunk, ROWS)] = solved
        return solved

    def wait_weights(slot):
        loads[slot, 1].wait()
        halves[slot].wait_recv()

    loads[1, 0].wait()

    @pl.when(depth != 0)
    def _():
        block_rows_copy.wait()

    @pl.when(depth == 4)
    def _():
        own_low.start()
        halves[1].start()
        loads[1, 2].wait()
        start_turn()
        for chunk in range(CHUNKS):
            set_reduced(1, chunk, None)
        halves[0].start()
        wait_ready()

    @pl.when(jnp.logical_and(depth != 0, depth != 4))
    def _():
        halves[1].start()
        halves[0].start()
        wait_ready()

    for level in range(LEVELS):
        if level < 3:
            @pl.when(depth == 4)
            def _():
                if level == 0:
                    pass_turn(1)
                    wait_weights(1)
                    fuse(0)
                    pass_turn(2)
                    fuse(1)
                elif level == 1:
                    fuse(2)
                    pass_turn(3)
                else:
                    fuse(3)
                    pass_turn(4)
                for chunk in range(CHUNKS):
                    if level < 2:
                        whole(chunk, 16, pass_send.at[level], ring_recv.at[level, chunk]).wait_recv()
                        each_hop(level, lambda where, which: hop(level, chunk, where, which).start())
                    else:
                        hop(level, chunk, leaf, 0).wait_recv()
                        spread(level, chunk)
                if level == 2:
                    fuse(4)
                    for chunk in range(CHUNKS):
                        solve(1, chunk)

            @pl.when(jnp.logical_and(depth != level, depth != 4))
            def _():
                for chunk in range(CHUNKS):
                    hop(level, chunk, leaf, 0).wait_recv()
                    start_ring(level, chunk)
                    start_hops(level, chunk)

                if level < 2:
                    @pl.when(depth == 3)
                    def _():
                        for chunk in range(CHUNKS):
                            wait_ring(level, chunk)
                            pass_down(level, chunk, child_a).start()
                            pass_down(level, chunk, child_b).start()
        else:
            @pl.when(depth != level)
            def _():
                for chunk in range(CHUNKS):
                    hop(level, chunk, leaf, 0).wait_recv()
                    start_ring(level, chunk)
                    start_hops(level, chunk)

        @pl.when(depth == level)
        def _():
            if level == 4:
                for chunk in range(CHUNKS):
                    wait_ring(2, chunk)
                    wait_ring(3, chunk)
                    rows = pl.ds(ROWS * chunk, ROWS)
                    solved = result[1, rows] - jnp.dot(
                        picked_of(1, chunk, 63), fused[...], preferred_element_type=F32
                    )
                    result[1, rows] = solved
                    rounded = solved.astype(BF16)
                    last[chunk, 2 * row] = rounded[:, :128]
                    last[chunk, 2 * row + 1] = rounded[:, 128:]
                    spread(level, chunk)
                return
            if level > 0:
                loads[1, 2].wait()
            for chunk in range(CHUNKS):
                for above in range(2 if level == 3 else 0, level):
                    wait_ring(above, chunk)
                set_reduced(1, chunk, offset_of(1, chunk, 16 * level - 1) if level else None)
            if level == 0:
                halves[1].start()
            wait_weights(1)
            for chunk in range(CHUNKS):
                rounded = solve(1, chunk).astype(BF16)
                anc[chunk][16 * level + 2 * row] = rounded[:, :128]
                anc[chunk][16 * level + 2 * row + 1] = rounded[:, 128:]
                if level == 0 and chunk == 0:
                    wait_ready()
                start_hops(level, chunk)
            for chunk in range(CHUNKS):
                start_ring(level, chunk)
            if level == 0:
                halves[0].start()
                loads[1, 2].wait()
                block_rows_copy.wait()

    @pl.when(depth < 0)
    def _():
        wait_weights(1)
        loads[1, 2].wait()
        result[1] = jnp.zeros_like(result[1])

    loads[0, 0].wait()
    loads[0, 2].wait()
    wait_weights(0)
    for chunk in range(CHUNKS):
        for level in range(LEVELS):
            @pl.when(depth <= level)
            def _():
                wait_ring(level, chunk)

        for block in range(16):
            anc[chunk][64 + block] = last[chunk, block]
        set_reduced(0, chunk, offset_of(0, chunk, 79))
    for chunk in range(CHUNKS):
        solve(0, chunk)

    halves[1].wait_send()
    halves[0].wait_send()

    for level in range(LEVELS):
        each_hop(
            level,
            lambda where, which: whole(
                0, 2 * CHUNKS, hop_send.at[level, which], hop_recv.at[level, 0]
            ).wait_send(),
        )
    for chunk in range(CHUNKS):
        for is_fused, levels in ((True, 3), (False, LEVELS)):
            @pl.when((depth == 4) == is_fused)
            def _():
                whole(chunk, levels * OTHERS, ring_send.at[chunk], ring_recv.at[0, chunk]).wait_send()

    @pl.when(depth == 3)
    def _():
        for level in range(2):
            part = low.at[0, pl.ds(0, 8)]
            remote(
                part, part, pass_send.at[level], ring_recv.at[level, 0], device(child_a, row, core)
            ).wait_send()

    @pl.when(depth == 4)
    def _():
        for side in range(2):
            part = low.at[:, pl.ds(0, 14)]
            remote(
                part, part, turn_send.at[side], turn_recv.at[0, side], device(leaf, row, 1 - core)
            ).wait_send()
        part = full.at[pl.ds(0, 7), own_half]
        remote(
            part, part, across_send.at[0], across_recv.at[0], device(leaf, row, 1 - core)
        ).wait_send()

    whole(0, CHUNKS * OTHERS, red_send.at[0], red_recv.at[0, 0]).wait_send()

    @pl.when(has_upper)
    def _():
        whole(0, CHUNKS * OTHERS, red_send.at[1], red_recv.at[1, 0]).wait_send()


def local(right_side, inverse_diag, lower_blocks, block_rows):
    anywhere = pl.BlockSpec(memory_space=pl.ANY)
    dma = pltpu.SemaphoreType.DMA
    return pl.pallas_call(
        kernel,
        name="sweep",
        out_shape=pltpu.VMEM((2, 64, 256), F32),
        in_specs=[anywhere] * 4,
        out_specs=pl.BlockSpec(memory_space=pltpu.VMEM),
        scratch_shapes=[
            pltpu.SMEM((2, 16), jnp.int32),
            pltpu.VMEM((2, 64, 256), F32),
            pltpu.VMEM((2, 2048, 256), BF16),
            pltpu.VMEM((2, 16, 128, 256), BF16),
            pltpu.VMEM((80, ROWS, 128), BF16),
            pltpu.VMEM((80, ROWS, 128), BF16),
            pltpu.VMEM((80, ROWS, 128), BF16),
            pltpu.VMEM((80, ROWS, 128), BF16),
            pltpu.VMEM((CHUNKS, 16, ROWS, 128), BF16),
            pltpu.VMEM((2, CHUNKS, 16, ROWS, 128), BF16),
            pltpu.VMEM((RING, 16, 128, 256), BF16),
            pltpu.VMEM((2048, 256), BF16),
            pltpu.VMEM((2048, 256), F32),
            dma((2, 3)),
            dma((2,)),
            dma((2,)),
            dma((2,)),
            dma((2, CHUNKS)),
            dma((LEVELS, 2)),
            dma((LEVELS, CHUNKS)),
            dma((CHUNKS,)),
            dma((LEVELS, CHUNKS)),
            dma((1,)),
            dma((2,)),
            dma((2,)),
            dma((4, 2, 2)),
            dma((1,)),
            dma((5,)),
            pltpu.SemaphoreType.REGULAR,
        ],
        compiler_params=pltpu.CompilerParams(
            collective_id=0, has_side_effects=True, vmem_limit_bytes=56 * 2**20
        ),
    )(block_rows, right_side, inverse_diag, lower_blocks)


def solution(mesh):
    return jax.shard_map(
        local,
        mesh=mesh,
        in_specs=(
            P("leaf", "rhs", "rows"),
            P("leaf", None, ("rows", "rhs")),
            P("leaf", None, None, "rows"),
            P("leaf", None),
        ),
        out_specs=P("leaf", "rhs", "rows"),
        check_vma=False,
    )
```

```python
import jax
import jax.numpy as jnp
from jax import lax
from jax.experimental import pallas as pl
from jax.experimental.pallas import tpu as pltpu
from jax.sharding import PartitionSpec as P

MESH = pl.DeviceIdType.MESH
BF16 = jnp.bfloat16
F32 = jnp.float32
RING = 8
LEVELS = 5
CHUNKS = 4
ROWS = 16
FAR_FIRST = (4, 3, 5, 2, 6, 1, 7)
OTHERS = 2 * len(FAR_FIRST)


def device(leaf, row, core):
    return {"leaf": leaf, "rows": row, "rhs": core}


def remote(source, target, sent, arrived, where):
    return pltpu.make_async_remote_copy(
        source, target, sent, arrived, device_id=where, device_id_type=MESH
    )


def depth_of(leaf):
    trail = jnp.int32(0)
    for power in range(1, 6):
        trail = trail + ((leaf + 1) % 2**power == 0).astype(jnp.int32)
    return 4 - trail


def kernel(
    block_rows_in, right_side, inverse_diag, lower_blocks, result,
    block_rows, rhs, inv, low, anc_0, anc_1, anc_2, anc_3, last, red, full, fused, total,
    load_sem, half_send, half_recv, red_send, red_recv, hop_send, hop_recv,
    ring_send, ring_recv, rows_sem, pass_send, turn_send, turn_recv, across_send, across_recv, ready,
):
    anc = (anc_0, anc_1, anc_2, anc_3,)
    leaf = lax.axis_index("leaf")
    row = lax.axis_index("rows")
    core = lax.axis_index("rhs")
    even = leaf % 2 == 0
    depth = depth_of(leaf)
    half_span = jnp.int32(0)
    for level in range(4):
        half_span = half_span + jnp.where(depth == level, 2 ** (3 - level), 0)
    span = jnp.maximum(2 * half_span, 1)
    parent = jnp.where((leaf // (2 * span)) % 2 == 0, leaf + span, leaf - span)
    child_a = leaf - half_span
    child_b = leaf + half_span
    has_upper = depth >= 0
    below_root = depth >= 1
    splits = jnp.logical_and(has_upper, depth <= 3)
    sibling = jnp.where(even, leaf + 1, leaf - 1)
    sibling_depth = depth_of(sibling)
    mine_cols = pl.ds(pl.multiple_of(core * 128, 128), 128)

    barrier = pltpu.get_barrier_semaphore()

    def greet(where):
        pl.semaphore_signal(barrier, inc=1, device_id=where, device_id_type=MESH)

    def report(where):
        pl.semaphore_signal(ready, inc=1, device_id=where, device_id_type=MESH)

    for step in FAR_FIRST:
        greet(device(leaf, (row + step) % RING, core))
    greet(device(leaf, row, 1 - core))

    @pl.when(splits)
    def _():
        greet(device(child_a, row, core))
        greet(device(child_b, row, core))

    @pl.when(even)
    def _():
        greet(device(sibling, row, core))

    block_rows_copy = pltpu.make_async_copy(block_rows_in, block_rows, rows_sem.at[0])
    loads = {}
    for slot in (1, 0):
        loads[slot, 0] = pltpu.make_async_copy(right_side.at[slot], rhs.at[slot], load_sem.at[slot, 0])
        loads[slot, 1] = pltpu.make_async_copy(
            inverse_diag.at[slot], inv.at[slot, :, mine_cols], load_sem.at[slot, 1]
        )
        loads[slot, 2] = pltpu.make_async_copy(lower_blocks.at[slot], low.at[slot], load_sem.at[slot, 2])
    for copy in loads.values():
        copy.start()
    block_rows_copy.start()

    pl.semaphore_wait(barrier, 8 + below_root.astype(jnp.int32) + jnp.where(even, 0, 1))

    @pl.when(below_root)
    def _():
        report(device(parent, row, core))

    @pl.when(jnp.logical_not(even))
    def _():
        report(device(sibling, row, core))

    def wait_ready():
        @pl.when(has_upper)
        def _():
            pl.semaphore_wait(ready, jnp.where(even, 1, 2))

    halves = {
        slot: remote(
            inverse_diag.at[slot], inv.at[slot, :, mine_cols], half_send.at[slot], half_recv.at[slot],
            device(leaf, row, 1 - core),
        )
        for slot in (1, 0)
    }

    def piece_at(level, chunk):
        if level == 4:
            return last.at[chunk, pl.ds(2 * row, 2)]
        return anc[chunk].at[pl.ds(16 * level + 2 * row, 2)]

    def ring_copies(level, chunk):
        piece = piece_at(level, chunk)
        return [
            remote(
                piece, piece, ring_send.at[chunk], ring_recv.at[level, chunk],
                device(leaf, (row + step) % RING, core),
            )
            for step in FAR_FIRST
        ]

    def red_copies(slot, chunk):
        piece = red.at[slot, chunk, pl.ds(2 * row, 2)]
        return [
            remote(
                piece, piece, red_send.at[slot], red_recv.at[slot, chunk],
                device(leaf, (row + step) % RING, core),
            )
            for step in FAR_FIRST
        ]

    def whole(chunk, blocks, sent, arrived):
        part = anc[chunk].at[pl.ds(0, blocks)]
        return remote(part, part, sent, arrived, device(leaf, row, 1 - core))

    def wait_ring(level, chunk):
        whole(chunk, OTHERS, ring_send.at[chunk], ring_recv.at[level, chunk]).wait_recv()

    def wait_red(slot, chunk):
        whole(chunk, OTHERS, red_send.at[slot], red_recv.at[slot, chunk]).wait_recv()

    def hop(level, chunk, where, which):
        piece = piece_at(level, chunk)
        return remote(
            piece, piece, hop_send.at[level, which], hop_recv.at[level, chunk],
            device(where, row, core),
        )

    def each_hop(level, act):
        if level < 4:
            @pl.when(jnp.logical_and(depth >= level, depth <= (3 if level >= 2 else 2)))
            def _():
                act(child_a, 0)
                act(child_b, 1)

        @pl.when(jnp.logical_and(even, sibling_depth < level))
        def _():
            act(sibling, 0)

    def start_hops(level, chunk):
        each_hop(level, lambda where, which: hop(level, chunk, where, which).start())

    def start_ring(level, chunk):
        for copy in ring_copies(level, chunk):
            copy.start()

    def spread(level, chunk):
        start_hops(level, chunk)
        start_ring(level, chunk)

    own_half = pl.ds(8 * core, 8)
    quarters = (pl.ds(8 * core, 4), pl.ds(8 * core + 4, 4))

    def turn(step, way, sub):
        piece = (row + RING - way * (step - 1)) % RING
        blocks = quarters[sub]
        source = low.at[1, blocks] if step == 1 else full.at[piece, blocks]
        side = 0 if way == 1 else 1
        return remote(
            source, full.at[piece, blocks], turn_send.at[side], turn_recv.at[step - 1, side, sub],
            device(leaf, (row + RING + way) % RING, core),
        )

    def travels(step, side, sub):
        return step < 4 or side == sub

    def start_turn():
        for sub in range(2):
            for way in (1, -1):
                turn(1, way, sub).start()

    def pass_turn(step):
        for sub in range(2):
            for way, side in ((1, 0), (-1, 1)):
                if not travels(step, side, sub):
                    continue
                piece = (row + RING - way * step) % RING
                turn(step, way, sub).wait_recv()
                if step < 4 and travels(step + 1, side, sub):
                    turn(step + 1, way, sub).start()
                blocks = full.at[piece, quarters[sub]]
                remote(
                    blocks, blocks, across_send.at[0], across_recv.at[step - 1],
                    device(leaf, row, 1 - core),
                ).start()

    def fuse(step):
        if step == 0:
            own_low.wait()
            pieces = [row]
        elif step < 4:
            pieces = [(row + step) % RING, (row + RING - step) % RING]
        else:
            pieces = [(row + step) % RING]
        if step:
            part = full.at[pl.ds(0, len(pieces)), own_half]
            remote(
                part, part, across_send.at[0], across_recv.at[step - 1], device(leaf, row, 1 - core)
            ).wait_recv()

        @pl.loop(0, 8)
        def _(tile):
            rows = pl.ds(pl.multiple_of(256 * tile, 256), 256)
            product = None
            for piece in pieces:
                term = jnp.dot(
                    full[piece, pl.ds(2 * tile, 2)].reshape(256, 256),
                    inv[1, pl.ds(pl.multiple_of(256 * piece, 256), 256)],
                    preferred_element_type=F32,
                )
                product = term if product is None else product + term
            if step:
                product = total[rows, :] + product
            if step < 4:
                total[rows, :] = product
            else:
                fused[rows, :] = product.astype(BF16)

    own_low = pltpu.make_async_copy(lower_blocks.at[1], full.at[row], across_recv.at[4])

    def pass_down(level, chunk, where):
        blocks = anc[chunk].at[pl.ds(16 * level, 16)]
        return remote(
            blocks, blocks, pass_send.at[level], ring_recv.at[level, chunk],
            device(where, row, core),
        )

    def set_reduced(slot, chunk, offset):
        span_rows = pl.ds(ROWS * chunk, ROWS)
        value = rhs[slot, span_rows]
        if offset is not None:
            value = value - offset
        rounded = value.astype(BF16)
        red[slot, chunk, 2 * row] = rounded[:, :128]
        red[slot, chunk, 2 * row + 1] = rounded[:, 128:]
        for copy in red_copies(slot, chunk):
            copy.start()

    def picked_of(slot, chunk, limit):
        return jnp.concatenate(
            [anc[chunk][jnp.clip(block_rows[slot, r], 0, limit)] for r in range(16)], axis=1
        )

    def offset_of(slot, chunk, limit):
        picked = picked_of(slot, chunk, limit)
        return jnp.dot(picked, low[slot].reshape(2048, 256), preferred_element_type=F32)

    def solve(slot, chunk):
        wait_red(slot, chunk)
        full = jnp.concatenate([red[slot, chunk, b] for b in range(16)], axis=1)
        solved = jnp.dot(full, inv[slot], preferred_element_type=F32)
        result[slot, pl.ds(ROWS * chunk, ROWS)] = solved
        return solved

    def wait_weights(slot):
        loads[slot, 1].wait()
        halves[slot].wait_recv()

    loads[1, 0].wait()

    @pl.when(depth != 0)
    def _():
        block_rows_copy.wait()

    @pl.when(depth == 4)
    def _():
        own_low.start()
        halves[1].start()
        loads[1, 2].wait()
        start_turn()
        halves[0].start()
        wait_ready()

    @pl.when(jnp.logical_and(depth != 0, depth != 4))
    def _():
        halves[1].start()
        halves[0].start()
        wait_ready()

    for level in range(LEVELS):
        if level < 3:
            @pl.when(depth == 4)
            def _():
                if level == 0:
                    pass_turn(1)
                    for chunk in range(CHUNKS):
                        set_reduced(1, chunk, None)
                    wait_weights(1)
                    fuse(0)
                    pass_turn(2)
                    fuse(1)
                elif level == 1:
                    fuse(2)
                    pass_turn(3)
                else:
                    fuse(3)
                    pass_turn(4)
                for chunk in range(CHUNKS):
                    if level < 2:
                        whole(chunk, 16, pass_send.at[level], ring_recv.at[level, chunk]).wait_recv()
                        each_hop(level, lambda where, which: hop(level, chunk, where, which).start())
                    else:
                        hop(level, chunk, leaf, 0).wait_recv()
                        spread(level, chunk)
                if level == 2:
                    fuse(4)
                    for chunk in range(CHUNKS):
                        solve(1, chunk)

            @pl.when(jnp.logical_and(depth != level, depth != 4))
            def _():
                for chunk in range(CHUNKS):
                    hop(level, chunk, leaf, 0).wait_recv()
                    start_ring(level, chunk)
                    start_hops(level, chunk)

                if level < 2:
                    @pl.when(depth == 3)
                    def _():
                        for chunk in range(CHUNKS):
                            wait_ring(level, chunk)
                            pass_down(level, chunk, child_a).start()
                            pass_down(level, chunk, child_b).start()
        else:
            @pl.when(depth != level)
            def _():
                for chunk in range(CHUNKS):
                    hop(level, chunk, leaf, 0).wait_recv()
                    start_ring(level, chunk)
                    start_hops(level, chunk)

        @pl.when(depth == level)
        def _():
            if level == 4:
                for chunk in range(CHUNKS):
                    wait_ring(2, chunk)
                    wait_ring(3, chunk)
                    rows = pl.ds(ROWS * chunk, ROWS)
                    solved = result[1, rows] - jnp.dot(
                        picked_of(1, chunk, 63), fused[...], preferred_element_type=F32
                    )
                    result[1, rows] = solved
                    rounded = solved.astype(BF16)
                    last[chunk, 2 * row] = rounded[:, :128]
                    last[chunk, 2 * row + 1] = rounded[:, 128:]
                    spread(level, chunk)
                return
            if level > 0:
                loads[1, 2].wait()
            for chunk in range(CHUNKS):
                for above in range(2 if level == 3 else 0, level):
                    wait_ring(above, chunk)
                set_reduced(1, chunk, offset_of(1, chunk, 16 * level - 1) if level else None)
            if level == 0:
                halves[1].start()
            wait_weights(1)
            for chunk in range(CHUNKS):
                rounded = solve(1, chunk).astype(BF16)
                anc[chunk][16 * level + 2 * row] = rounded[:, :128]
                anc[chunk][16 * level + 2 * row + 1] = rounded[:, 128:]
                if level == 0 and chunk == 0:
                    wait_ready()
                start_hops(level, chunk)
            for chunk in range(CHUNKS):
                start_ring(level, chunk)
            if level == 0:
                halves[0].start()
                loads[1, 2].wait()
                block_rows_copy.wait()

    @pl.when(depth < 0)
    def _():
        wait_weights(1)
        loads[1, 2].wait()
        result[1] = jnp.zeros_like(result[1])

    loads[0, 0].wait()
    loads[0, 2].wait()
    wait_weights(0)
    for chunk in range(CHUNKS):
        for level in range(LEVELS):
            @pl.when(depth <= level)
            def _():
                wait_ring(level, chunk)

        for block in range(16):
            anc[chunk][64 + block] = last[chunk, block]
        set_reduced(0, chunk, offset_of(0, chunk, 79))
    for chunk in range(CHUNKS):
        solve(0, chunk)

    halves[1].wait_send()
    halves[0].wait_send()

    for level in range(LEVELS):
        each_hop(
            level,
            lambda where, which: whole(
                0, 2 * CHUNKS, hop_send.at[level, which], hop_recv.at[level, 0]
            ).wait_send(),
        )
    for chunk in range(CHUNKS):
        for is_fused, levels in ((True, 3), (False, LEVELS)):
            @pl.when((depth == 4) == is_fused)
            def _():
                whole(chunk, levels * OTHERS, ring_send.at[chunk], ring_recv.at[0, chunk]).wait_send()

    @pl.when(depth == 3)
    def _():
        for level in range(2):
            part = low.at[0, pl.ds(0, 8)]
            remote(
                part, part, pass_send.at[level], ring_recv.at[level, 0], device(child_a, row, core)
            ).wait_send()

    @pl.when(depth == 4)
    def _():
        for side in range(2):
            part = low.at[:, pl.ds(0, 14)]
            remote(
                part, part, turn_send.at[side], turn_recv.at[0, side], device(leaf, row, 1 - core)
            ).wait_send()
        part = full.at[pl.ds(0, 7), own_half]
        remote(
            part, part, across_send.at[0], across_recv.at[0], device(leaf, row, 1 - core)
        ).wait_send()

    whole(0, CHUNKS * OTHERS, red_send.at[0], red_recv.at[0, 0]).wait_send()

    @pl.when(has_upper)
    def _():
        whole(0, CHUNKS * OTHERS, red_send.at[1], red_recv.at[1, 0]).wait_send()


def local(right_side, inverse_diag, lower_blocks, block_rows):
    anywhere = pl.BlockSpec(memory_space=pl.ANY)
    dma = pltpu.SemaphoreType.DMA
    return pl.pallas_call(
        kernel,
        name="sweep",
        out_shape=pltpu.VMEM((2, 64, 256), F32),
        in_specs=[anywhere] * 4,
        out_specs=pl.BlockSpec(memory_space=pltpu.VMEM),
        scratch_shapes=[
            pltpu.SMEM((2, 16), jnp.int32),
            pltpu.VMEM((2, 64, 256), F32),
            pltpu.VMEM((2, 2048, 256), BF16),
            pltpu.VMEM((2, 16, 128, 256), BF16),
            pltpu.VMEM((80, ROWS, 128), BF16),
            pltpu.VMEM((80, ROWS, 128), BF16),
            pltpu.VMEM((80, ROWS, 128), BF16),
            pltpu.VMEM((80, ROWS, 128), BF16),
            pltpu.VMEM((CHUNKS, 16, ROWS, 128), BF16),
            pltpu.VMEM((2, CHUNKS, 16, ROWS, 128), BF16),
            pltpu.VMEM((RING, 16, 128, 256), BF16),
            pltpu.VMEM((2048, 256), BF16),
            pltpu.VMEM((2048, 256), F32),
            dma((2, 3)),
            dma((2,)),
            dma((2,)),
            dma((2,)),
            dma((2, CHUNKS)),
            dma((LEVELS, 2)),
            dma((LEVELS, CHUNKS)),
            dma((CHUNKS,)),
            dma((LEVELS, CHUNKS)),
            dma((1,)),
            dma((2,)),
            dma((2,)),
            dma((4, 2, 2)),
            dma((1,)),
            dma((5,)),
            pltpu.SemaphoreType.REGULAR,
        ],
        compiler_params=pltpu.CompilerParams(
            collective_id=0, has_side_effects=True, vmem_limit_bytes=56 * 2**20
        ),
    )(block_rows, right_side, inverse_diag, lower_blocks)


def solution(mesh):
    return jax.shard_map(
        local,
        mesh=mesh,
        in_specs=(
            P("leaf", "rhs", "rows"),
            P("leaf", None, ("rows", "rhs")),
            P("leaf", None, None, "rows"),
            P("leaf", None),
        ),
        out_specs=P("leaf", "rhs", "rows"),
        check_vma=False,
    )
```
